32 devices in a mesh: dp: 8 (over z, x), mp: 4 (over y, core).
Axes of the slice: x: 2, y: 2, z: 4, core: 2. Of those that a mesh axis runs over, the one named last changes fastest.
Arguments:
- source_ids: int32 [2, 8, 1024], P(None, 'dp'), may hold values from 0 to 383
- target_ids: int32 [2, 8, 256], P(None, 'dp'), may hold values from 0 to 383
- source_lengths: int32 [2, 8], P(None, 'dp'), may hold values from 512 to 1024
- target_lengths: int32 [2, 8], P(None, 'dp'), may hold values from 64 to 256
- embedding: float32 [384, 1536], P('mp', 'dp'), may hold values from -6 to 6
- unembedding: float32 [1536, 384], P('dp', 'mp'), may hold values from -0.3125 to 0.3125
- attention_in: float32 [3, 1536, 3, 768], P(None, 'dp', None, 'mp'), may hold values from -0.15625 to 0.15625
- attention_out: float32 [3, 768, 1536], P(None, 'mp', 'dp'), may hold values from -1.75 to 1.75
- feed_in: float32 [2, 1536, 2, 3968], P(None, 'dp', None, 'mp'), may hold values from -0.15625 to 0.15625
- feed_out: float32 [2, 3968, 1536], P(None, 'mp', 'dp'), may hold values from -0.09375 to 0.09375
- norm_gains: float32 [7, 1536], P(None, ('dp', 'mp')), may hold values from 0.5 to 1.5
- embedding_first: float32 [384, 1536], P('mp', 'dp'), may hold values from -1.4305115e-06 to 1.4305115e-06
- unembedding_first: float32 [1536, 384], P('dp', 'mp'), may hold values from -4.7683716e-06 to 4.7683716e-06
- attention_in_first: float32 [3, 1536, 3, 768], P(None, 'dp', None, 'mp'), may hold values from -4.7683716e-06 to 4.7683716e-06
- attention_out_first: float32 [3, 768, 1536], P(None, 'mp', 'dp'), may hold values from -4.7683716e-06 to 4.7683716e-06
- feed_in_first: float32 [2, 1536, 2, 3968], P(None, 'dp', None, 'mp'), may hold values from -4.7683716e-06 to 4.7683716e-06
- feed_out_first: float32 [2, 3968, 1536], P(None, 'mp', 'dp'), may hold values from -4.7683716e-06 to 4.7683716e-06
- norm_gains_first: float32 [7, 1536], P(None, ('dp', 'mp')), may hold values from -4.7683716e-06 to 4.7683716e-06
- embedding_second: float32 [384, 1536], P('mp', 'dp'), may hold values from 5.7786472e-15 to 2.3114589e-14
- unembedding_second: float32 [1536, 384], P('dp', 'mp'), may hold values from 4.8155395e-14 to 1.9262158e-13
- attention_in_second: float32 [3, 1536, 3, 768], P(None, 'dp', None, 'mp'), may hold values from 4.8155395e-14 to 1.9262158e-13
- attention_out_second: float32 [3, 768, 1536], P(None, 'mp', 'dp'), may hold values from 4.8155395e-14 to 1.9262158e-13
- feed_in_second: float32 [2, 1536, 2, 3968], P(None, 'dp', None, 'mp'), may hold values from 4.8155395e-14 to 1.9262158e-13
- feed_out_second: float32 [2, 3968, 1536], P(None, 'mp', 'dp'), may hold values from 4.8155395e-14 to 1.9262158e-13
- norm_gains_second: float32 [7, 1536], P(None, ('dp', 'mp')), may hold values from 4.8155395e-14 to 1.9262158e-13
Outputs:
- loss: float32 [], replicated
- grad_norm: float32 [], replicated
- new_embedding: float32 [384, 1536], P('mp', 'dp')
- new_unembedding: float32 [1536, 384], P('dp', 'mp')
- new_attention_in: float32 [3, 1536, 3, 768], P(None, 'dp', None, 'mp')
- new_attention_out: float32 [3, 768, 1536], P(None, 'mp', 'dp')
- new_feed_in: float32 [2, 1536, 2, 3968], P(None, 'dp', None, 'mp')
- new_feed_out: float32 [2, 3968, 1536], P(None, 'mp', 'dp')
- new_norm_gains: float32 [7, 1536], P(None, ('dp', 'mp'))
- new_embedding_first: float32 [384, 1536], P('mp', 'dp')
- new_unembedding_first: float32 [1536, 384], P('dp', 'mp')
- new_attention_in_first: float32 [3, 1536, 3, 768], P(None, 'dp', None, 'mp')
- new_attention_out_first: float32 [3, 768, 1536], P(None, 'mp', 'dp')
- new_feed_in_first: float32 [2, 1536, 2, 3968], P(None, 'dp', None, 'mp')
- new_feed_out_first: float32 [2, 3968, 1536], P(None, 'mp', 'dp')
- new_norm_gains_first: float32 [7, 1536], P(None, ('dp', 'mp'))
- new_embedding_second: float32 [384, 1536], P('mp', 'dp')
- new_unembedding_second: float32 [1536, 384], P('dp', 'mp')
- new_attention_in_second: float32 [3, 1536, 3, 768], P(None, 'dp', None, 'mp')
- new_attention_out_second: float32 [3, 768, 1536], P(None, 'mp', 'dp')
- new_feed_in_second: float32 [2, 1536, 2, 3968], P(None, 'dp', None, 'mp')
- new_feed_out_second: float32 [2, 3968, 1536], P(None, 'mp', 'dp')
- new_norm_gains_second: float32 [7, 1536], P(None, ('dp', 'mp'))
The draws below stay inside these ranges and needn't reach their ends.
All inputs are finite; a program needn't handle non-finite values.
Results may differ from the reference program's by a relative error of at most 0.02.
Values may be sent and summed in bfloat16 or wider, within the bound.
No kernel may reach another device: no remote copies, remote signals or barrier semaphores. Data moves between devices by JAX's collectives and lax.ppermute only.
A program may use at most 384 MiB of HBM per device.

```python
import math
import jax
import jax.numpy as jnp
from jax import lax

D = 1536
H = 12
DK = 64
FF = 3968
V = 384
SRC = 1024
TGT = 256
MICRO = 2
STEP = 10
HD = 768
BATCH = 8
PARAMS = 51915264


def plant(result, stream_key, low, top_value):
    shape = result.shape
    index_at = [jax.random.randint(jax.random.fold_in(stream_key, axis), (), 0, shape[axis]) for axis in range(len(shape))]
    result = result.at[tuple(index_at)].set(low)
    longest = shape.index(max(shape))
    index_at[longest] = (index_at[longest] + 1) % shape[longest]
    return result.at[tuple(index_at)].set(top_value)


def level_of(stream_key, shape, cuts, low, largest):
    def one(position, shards_of):
        steps = jax.random.uniform(jax.random.fold_in(jax.random.fold_in(stream_key, 6), position), (shards_of,), jnp.float32, low / len(cuts), largest / len(cuts))
        return jnp.repeat(jnp.exp(steps), shape[position] // shards_of).reshape((-1,) + (1,) * (len(shape) - position - 1))

    level = one(*cuts[0])
    for cut in cuts[1:]:
        level = level * one(*cut)
    return level


def scatter_about(own_key, extent, deviation, most, cuts=(), kind=jnp.bfloat16):
    level = level_of(own_key, extent, cuts, -0.22, 0.18) if cuts else 1.0
    entries = jax.random.normal(own_key, extent, jnp.float32) * deviation * level
    return jnp.minimum(jnp.maximum(entries, -most), most).astype(kind)


def setup_inputs(seed: int = 0) -> dict:
    keys = jax.random.split(jax.random.key(seed), 26)
    source_ids = plant(jax.random.randint(keys[0], (MICRO, BATCH, SRC), 0, V), jax.random.fold_in(keys[0], 1), 0, V - 1).astype(jnp.int32)
    target_ids = plant(jax.random.randint(keys[1], (MICRO, BATCH, TGT), 0, V), jax.random.fold_in(keys[1], 1), 0, V - 1).astype(jnp.int32)
    source_lengths = plant(jax.random.randint(keys[2], (MICRO, BATCH), SRC // 2, SRC + 1), jax.random.fold_in(keys[2], 1), SRC // 2, SRC).astype(jnp.int32)
    target_lengths = plant(jax.random.randint(keys[3], (MICRO, BATCH), TGT // 4, TGT + 1), jax.random.fold_in(keys[3], 1), TGT // 4, TGT).astype(jnp.int32)
    embedding = scatter_about(keys[4], (V, D), 1.0, 6.0, ((0, 4), (1, 8)), jnp.float32)
    unembedding = scatter_about(keys[5], (D, V), (D // 4) ** -0.5, 0.3125, ((0, 8), (1, 4)), jnp.float32)
    attention_in = scatter_about(keys[6], (3, D, 3, HD), D ** -0.5, 0.15625, ((1, 8), (3, 4)), jnp.float32)
    attention_out = scatter_about(keys[7], (3, HD, D), (max(HD // 64, 1)) ** -0.5, 1.75, ((1, 4), (2, 8)), jnp.float32)
    feed_in = scatter_about(keys[8], (2, D, 2, FF), D ** -0.5, 0.15625, ((1, 8), (3, 4)), jnp.float32)
    feed_out = scatter_about(keys[9], (2, FF, D), FF ** -0.5, 0.09375, ((1, 4), (2, 8)), jnp.float32)
    norm_gains = jnp.clip(1.0 + 0.1 * jax.random.normal(keys[10], (7, D), jnp.float32), 0.5, 1.5)
    embedding_first = scatter_about(keys[11], (V, D), (0.0016 / PARAMS ** 0.5), 1.430511474609375e-06, ((0, 4), (1, 8)), jnp.float32)
    unembedding_first = scatter_about(keys[12], (D, V), (0.0056 / PARAMS ** 0.5), 4.76837158203125e-06, ((0, 8), (1, 4)), jnp.float32)
    attention_in_first = scatter_about(keys[13], (3, D, 3, HD), (0.0056 / PARAMS ** 0.5), 4.76837158203125e-06, ((1, 8), (3, 4)), jnp.float32)
    attention_out_first = scatter_about(keys[14], (3, HD, D), (0.0056 / PARAMS ** 0.5), 4.76837158203125e-06, ((1, 4), (2, 8)), jnp.float32)
    feed_in_first = scatter_about(keys[15], (2, D, 2, FF), (0.0056 / PARAMS ** 0.5), 4.76837158203125e-06, ((1, 8), (3, 4)), jnp.float32)
    feed_out_first = scatter_about(keys[16], (2, FF, D), (0.0056 / PARAMS ** 0.5), 4.76837158203125e-06, ((1, 4), (2, 8)), jnp.float32)
    norm_gains_first = scatter_about(keys[17], (7, D), (0.0056 / PARAMS ** 0.5), 4.76837158203125e-06, ((1, 32),), jnp.float32)
    embedding_second = jnp.clip(jnp.exp(math.log(2.3114588923998404e-14) - 1.3862944 * jax.random.uniform(keys[18], (V, D), jnp.float32) ** level_of(keys[18], (V, D), ((0, 4), (1, 8)), -0.2, 0.2)), 5.778647230999601e-15, 2.3114588923998404e-14)
    unembedding_second = jnp.clip(jnp.exp(math.log(1.9262158057822831e-13) - 1.3862944 * jax.random.uniform(keys[19], (D, V), jnp.float32) ** level_of(keys[19], (D, V), ((0, 8), (1, 4)), -0.2, 0.2)), 4.815539514455708e-14, 1.9262158057822831e-13)
    attention_in_second = jnp.clip(jnp.exp(math.log(1.9262158057822831e-13) - 1.3862944 * jax.random.uniform(keys[20], (3, D, 3, HD), jnp.float32) ** level_of(keys[20], (3, D, 3, HD), ((1, 8), (3, 4)), -0.2, 0.2)), 4.815539514455708e-14, 1.9262158057822831e-13)
    attention_out_second = jnp.clip(jnp.exp(math.log(1.9262158057822831e-13) - 1.3862944 * jax.random.uniform(keys[21], (3, HD, D), jnp.float32) ** level_of(keys[21], (3, HD, D), ((1, 4), (2, 8)), -0.2, 0.2)), 4.815539514455708e-14, 1.9262158057822831e-13)
    feed_in_second = jnp.clip(jnp.exp(math.log(1.9262158057822831e-13) - 1.3862944 * jax.random.uniform(keys[22], (2, D, 2, FF), jnp.float32) ** level_of(keys[22], (2, D, 2, FF), ((1, 8), (3, 4)), -0.2, 0.2)), 4.815539514455708e-14, 1.9262158057822831e-13)
    feed_out_second = jnp.clip(jnp.exp(math.log(1.9262158057822831e-13) - 1.3862944 * jax.random.uniform(keys[23], (2, FF, D), jnp.float32) ** level_of(keys[23], (2, FF, D), ((1, 4), (2, 8)), -0.2, 0.2)), 4.815539514455708e-14, 1.9262158057822831e-13)
    norm_gains_second = jnp.clip(jnp.exp(math.log(1.9262158057822831e-13) - 1.3862944 * jax.random.uniform(keys[24], (7, D), jnp.float32) ** level_of(keys[24], (7, D), ((1, 32),), -0.2, 0.2)), 4.815539514455708e-14, 1.9262158057822831e-13)
    return dict(source_ids=source_ids, target_ids=target_ids, source_lengths=source_lengths, target_lengths=target_lengths, embedding=embedding, unembedding=unembedding, attention_in=attention_in, attention_out=attention_out, feed_in=feed_in, feed_out=feed_out, norm_gains=norm_gains, embedding_first=embedding_first, unembedding_first=unembedding_first, attention_in_first=attention_in_first, attention_out_first=attention_out_first, feed_in_first=feed_in_first, feed_out_first=feed_out_first, norm_gains_first=norm_gains_first, embedding_second=embedding_second, unembedding_second=unembedding_second, attention_in_second=attention_in_second, attention_out_second=attention_out_second, feed_in_second=feed_in_second, feed_out_second=feed_out_second, norm_gains_second=norm_gains_second)


HIGH = lax.Precision.HIGHEST
norm_eps = 1e-06
clip_limit = 0.05
step_rates = (0.4, 0.02, 0.02, 0.1, 0.02, 0.02, 0.25)
beta_one = 0.9
beta_two = 0.999
adam_eps = 1e-08
decay = 0.01
masked = -1000000000.0

@jax.custom_vjp
def low(v):
    return lax.optimization_barrier(v.astype(jnp.bfloat16)).astype(jnp.float32)

@jax.custom_vjp
def low_back(v):
    return v

def low_keep(v):
    return (low(v), None)

def low_pass(kept, grad):
    return (grad,)

def back_keep(v):
    return (v, None)

def back_low(kept, grad):
    return (low(grad),)
low.defvjp(low_keep, low_pass)
low_back.defvjp(back_keep, back_low)

def rounded(v):
    return low(low_back(v))

def matmul(left, right):
    return jnp.dot(left, right, precision=HIGH)

def rms_norm(x, gain):
    return x * lax.rsqrt(lax.optimization_barrier(jnp.mean(x * x, axis=-1, keepdims=True)) + norm_eps) * gain

def attention(x_query, x_keys, w_in, w_out, bias):
    rows = x_query.shape[0]
    cols = x_keys.shape[0]
    query = rounded(matmul(x_query, w_in[:, 0])).reshape(rows, H, DK)
    key = rounded(matmul(x_keys, w_in[:, 1])).reshape(cols, H, DK)
    value = rounded(matmul(x_keys, w_in[:, 2])).reshape(cols, H, DK)
    scores = low_back(jnp.einsum('rhd,shd->hrs', query, key, precision=HIGH) * 0.125 + bias)
    peak = lax.optimization_barrier(jnp.max(scores, axis=-1, keepdims=True))
    raw = jnp.exp(scores - peak)
    probs = low(raw / lax.optimization_barrier(jnp.sum(raw, axis=-1, keepdims=True)))
    mixed = rounded(jnp.einsum('hrs,shd->rhd', probs, value, precision=HIGH).reshape(rows, H * DK))
    return low_back(matmul(mixed, w_out))

def feed_forward(x_in, w_in, w_out):
    gate = low_back(matmul(x_in, w_in[:, 0]))
    upper = low_back(matmul(x_in, w_in[:, 1]))
    hidden = low(jax.nn.gelu(gate, approximate=True) * upper)
    return low_back(matmul(hidden, w_out))

def sequence_loss(weights, gains, source, target, source_len, target_len, count):
    table, out_table, attn_in, attn_out, feed_in, feed_out = [low(w) for w in weights]
    src_pos = jnp.arange(SRC, dtype=jnp.int32)
    tgt_pos = jnp.arange(TGT, dtype=jnp.int32)
    key_bias = jnp.where(src_pos < source_len, 0.0, masked)[None, None, :]
    causal = jnp.where(tgt_pos[:, None] >= tgt_pos[None, :], 0.0, masked)[None]
    stream = low_back(table[source])
    normed = low(rms_norm(stream, gains[0]))
    stream = stream + attention(normed, normed, attn_in[0], attn_out[0], key_bias)
    stream = stream + feed_forward(low(rms_norm(stream, gains[1])), feed_in[0], feed_out[0])
    encoded = low(rms_norm(stream, gains[2]))
    shifted = jnp.concatenate([jnp.zeros((1,), jnp.int32), target[:-1].astype(jnp.int32)])
    dec = low_back(table[shifted])
    normed = low(rms_norm(dec, gains[3]))
    dec = dec + attention(normed, normed, attn_in[1], attn_out[1], causal)
    dec = dec + attention(low(rms_norm(dec, gains[4])), encoded, attn_in[2], attn_out[2], key_bias)
    dec = dec + feed_forward(low(rms_norm(dec, gains[5])), feed_in[1], feed_out[1])
    logits = low_back(matmul(low(rms_norm(dec, gains[6])), out_table))
    peak = lax.optimization_barrier(jnp.max(logits, axis=-1))
    total = peak + jnp.log(lax.optimization_barrier(jnp.sum(jnp.exp(logits - peak[:, None]), axis=-1)))
    picked = jnp.take_along_axis(logits, target[:, None].astype(jnp.int32), axis=1)[:, 0]
    weight = (tgt_pos < target_len).astype(jnp.float32)
    return jnp.sum((total - picked) * weight) / count

def adam(weight, grad, first, second, step_rate):
    first = beta_one * first + (1 - beta_one) * grad
    second = beta_two * second + (1 - beta_two) * grad * grad
    step_size = first / (1 - beta_one ** STEP) / (jnp.sqrt(second / (1 - beta_two ** STEP)) + adam_eps)
    return (weight - step_rate * (step_size + decay * weight), first, second)

def reference(source_ids, target_ids, source_lengths, target_lengths, embedding, unembedding, attention_in, attention_out, feed_in, feed_out, norm_gains, embedding_first, unembedding_first, attention_in_first, attention_out_first, feed_in_first, feed_out_first, norm_gains_first, embedding_second, unembedding_second, attention_in_second, attention_out_second, feed_in_second, feed_out_second, norm_gains_second):
    weights = (embedding, unembedding, attention_in, attention_out, feed_in, feed_out)
    firsts = (embedding_first, unembedding_first, attention_in_first, attention_out_first, feed_in_first, feed_out_first, norm_gains_first)
    seconds = (embedding_second, unembedding_second, attention_in_second, attention_out_second, feed_in_second, feed_out_second, norm_gains_second)
    count = jnp.sum(target_lengths).astype(jnp.float32)
    batches = (source_ids.reshape(-1, SRC), target_ids.reshape(-1, TGT), source_lengths.reshape(-1), target_lengths.reshape(-1))

    def one(carry, batch):
        grads, loss_sum = carry
        source, target, source_len, target_len = batch
        value, pull = jax.vjp(lambda w, g: sequence_loss(w, g, source, target, source_len, target_len, count), weights, norm_gains)
        got = pull(jnp.ones_like(value))
        grads = jax.tree.map(jnp.add, grads, got)
        return ((grads, loss_sum + value), None)
    init = (jax.tree.map(jnp.zeros_like, (weights, norm_gains)), jnp.zeros((), jnp.float32))
    (grads, loss), _ = lax.scan(one, init, batches)
    flat = list(grads[0]) + [grads[1]]
    grad_norm = jnp.sqrt(sum((jnp.sum(g * g) for g in flat)))
    scale = jnp.minimum(1.0, clip_limit / grad_norm)
    masters = list(weights) + [norm_gains]
    results = [adam(w, g * scale, m, v, r) for w, g, m, v, r in zip(masters, flat, firsts, seconds, step_rates)]
    news = tuple((r[0] for r in results))
    moms = tuple((r[1] for r in results))
    secs = tuple((r[2] for r in results))
    return (loss, grad_norm, news[0], news[1], news[2], news[3], news[4], news[5], news[6], moms[0], moms[1], moms[2], moms[3], moms[4], moms[5], moms[6], secs[0], secs[1], secs[2], secs[3], secs[4], secs[5], secs[6])
```

```python
import jax
import jax.numpy as jnp
import numpy as np
from jax import lax
from jax.sharding import Mesh
from jax.sharding import PartitionSpec as P

DK = 64
STEP = 10


norm_eps = 1e-06
clip_limit = 0.05
step_rates = (0.4, 0.02, 0.02, 0.1, 0.02, 0.02, 0.25)
beta_one = 0.9
beta_two = 0.999
adam_eps = 1e-08
decay = 0.01
masked = -1000000000.0

half = jnp.bfloat16


def spin(part, axis, shift):
    size = lax.axis_size(axis)
    return lax.ppermute(part, axis, [(i, (i + shift) % size) for i in range(size)])


def flip(part, axis, bit):
    size = lax.axis_size(axis)
    return lax.ppermute(part, axis, [(i, i ^ bit) for i in range(size)])


def gather_rows(part, axis):
    pieces = [part] + [spin(part, axis, k) for k in range(1, lax.axis_size(axis))]
    return jnp.concatenate(pieces, axis=0)


def scatter_rows(part, axis):
    size = lax.axis_size(axis)
    rows = part.shape[0] // size
    total = part[:rows].astype(jnp.float32)
    for k in range(1, size):
        total = total + spin(part[k * rows : (k + 1) * rows], axis, -k).astype(jnp.float32)
    return total


def gather_unit(part, axes, inner_first):
    for axis in axes[:-1]:
        part = gather_rows(part, axis)
    if inner_first:
        part = gather_rows(part, axes[-1])
        return [part, spin(part, "y", 1)]
    other = spin(part, "y", 1)
    return [gather_rows(part, axes[-1]), gather_rows(other, axes[-1])]


def meet(own, sent):
    return own.astype(jnp.float32) + spin(sent, "y", 1).astype(jnp.float32)


def scatter_unit(parts, axes, inner_first):
    if inner_first:
        part = scatter_rows(meet(parts[0], parts[1]).astype(half), axes[-1])
    else:
        own, sent = [scatter_rows(p, axes[-1]).astype(half) for p in parts]
        part = meet(own, sent)
    for axis in axes[:-1][::-1]:
        part = scatter_rows(part.astype(half), axis)
    return part


def total_over(value, axes):
    for axis in axes:
        bit = 1
        while bit < lax.axis_size(axis):
            value = value + flip(value, axis, bit)
            bit *= 2
    return value


def in_order(own, other, axis):
    first = lax.axis_index(axis) == 0
    return jnp.where(
        first, jnp.concatenate([own, other], axis=1), jnp.concatenate([other, own], axis=1)
    )


def collect(own):
    return jnp.concatenate([own, spin(own, "c", 1)], axis=0)


def fold(part):
    rows = part.shape[0] // 2
    return part[:rows] + spin(part[rows:].astype(half), "c", 1).astype(jnp.float32)


def product(left, right):
    return jnp.dot(left, right, preferred_element_type=jnp.float32)


def product_left(left, right):
    return lax.dot_general(
        left, right, (((0,), (0,)), ((), ())), preferred_element_type=jnp.float32
    )


def product_right(left, right):
    return lax.dot_general(
        left, right, (((1,), (1,)), ((), ())), preferred_element_type=jnp.float32
    )


def rms_norm(stream, gain):
    return stream * lax.rsqrt(jnp.mean(stream * stream, axis=-1, keepdims=True) + norm_eps) * gain


def normalize(stream, gain):
    return rms_norm(stream, gain).astype(half)


def norm_back(stream, gain, grad):
    _, pull = jax.vjp(rms_norm, stream, gain)
    return pull(grad)


def heads(flat):
    return flat.reshape(flat.shape[0], -1, DK)


def score_block(query, key, bias):
    return (
        jnp.einsum("rhd,shd->hrs", heads(query), heads(key), preferred_element_type=jnp.float32)
        * 0.125
        + bias
    )


def attend(query, key, value, bias):
    scores = score_block(query, key, bias)
    peak = jnp.max(scores, axis=-1, keepdims=True)
    raw = jnp.exp(scores - peak)
    total = jnp.sum(raw, axis=-1, keepdims=True)
    probs = (raw / total).astype(half)
    mixed = jnp.einsum("hrs,shd->rhd", probs, heads(value), preferred_element_type=jnp.float32)
    mixed = mixed.reshape(query.shape[0], -1).astype(half)
    return mixed, peak + jnp.log(total)


def attend_back(query, key, value, lse, bias, d_mixed):
    rows = query.shape[0]
    cols = key.shape[0]
    d_heads = heads(d_mixed)
    probs = jnp.exp(score_block(query, key, bias) - lse)
    d_value = jnp.einsum(
        "hrs,rhd->shd", probs.astype(half), d_heads, preferred_element_type=jnp.float32
    )
    d_probs = jnp.einsum("rhd,shd->hrs", d_heads, heads(value), preferred_element_type=jnp.float32)
    d_scores = (probs * (d_probs - jnp.sum(probs * d_probs, axis=-1, keepdims=True))).astype(half)
    d_query = (
        jnp.einsum("hrs,shd->rhd", d_scores, heads(key), preferred_element_type=jnp.float32) * 0.125
    )
    d_key = (
        jnp.einsum("hrs,rhd->shd", d_scores, heads(query), preferred_element_type=jnp.float32)
        * 0.125
    )
    return (
        d_query.reshape(rows, -1).astype(half),
        d_key.reshape(cols, -1).astype(half),
        d_value.reshape(cols, -1).astype(half),
    )


def self_attention(x_in, blocks, bias):
    part = 0.0
    kept = []
    for block in blocks:
        width = block.shape[1] // 4
        qkv = product(x_in, block[:, : 3 * width]).astype(half)
        query, key, value = qkv[:, :width], qkv[:, width : 2 * width], qkv[:, 2 * width :]
        mixed, lse = attend(query, key, value, bias)
        part = part + product_right(mixed, block[:, 3 * width :])
        kept.append((query, key, value, lse, mixed))
    return part, kept


def self_attention_back(x_in, blocks, bias, kept, d_full):
    d_in = 0.0
    grads = []
    for block, (query, key, value, lse, mixed) in zip(blocks, kept):
        width = block.shape[1] // 4
        g_out = product_left(d_full, mixed).astype(half)
        d_mixed = product(d_full, block[:, 3 * width :]).astype(half)
        d_qkv = jnp.concatenate(attend_back(query, key, value, lse, bias, d_mixed), axis=1)
        g_in = product_left(x_in, d_qkv).astype(half)
        grads.append(jnp.concatenate([g_in, g_out], axis=1))
        d_in = d_in + product_right(d_qkv, block[:, : 3 * width])
    return grads, d_in


def cross_attention(x_in, x_keys, blocks, bias):
    part = 0.0
    kept = []
    for block in blocks:
        width = block.shape[1] // 4
        query = product(x_in, block[:, :width]).astype(half)
        pair = product(x_keys, block[:, width : 3 * width]).astype(half)
        key, value = pair[:, :width], pair[:, width:]
        mixed, lse = attend(query, key, value, bias)
        part = part + product_right(mixed, block[:, 3 * width :])
        kept.append((query, key, value, lse, mixed))
    return part, kept


def cross_attention_back(x_in, x_keys, blocks, bias, kept, d_full):
    d_in = 0.0
    d_keys = 0.0
    grads = []
    for block, (query, key, value, lse, mixed) in zip(blocks, kept):
        width = block.shape[1] // 4
        g_out = product_left(d_full, mixed).astype(half)
        d_mixed = product(d_full, block[:, 3 * width :]).astype(half)
        d_query, d_key, d_value = attend_back(query, key, value, lse, bias, d_mixed)
        d_pair = jnp.concatenate([d_key, d_value], axis=1)
        g_query = product_left(x_in, d_query).astype(half)
        g_pair = product_left(x_keys, d_pair).astype(half)
        grads.append(jnp.concatenate([g_query, g_pair, g_out], axis=1))
        d_in = d_in + product_right(d_query, block[:, :width])
        d_keys = d_keys + product_right(d_pair, block[:, width : 3 * width])
    return grads, d_in, d_keys


def gated(gate, upper):
    return jax.nn.gelu(gate, approximate=True) * upper


def expand(x_in, gates, uppers, downs):
    part = 0.0
    kept = []
    for w_gate, w_upper, w_down in zip(gates, uppers, downs):
        gate = product(x_in, w_gate)
        upper = product(x_in, w_upper)
        hidden = gated(gate, upper).astype(half)
        part = part + product_right(hidden, w_down)
        kept.append((gate, upper, hidden))
    return part, kept


def expand_back(x_in, gates, uppers, downs, kept, d_full):
    d_in = 0.0
    g_gates, g_uppers, g_downs = [], [], []
    for w_gate, w_upper, w_down, (gate, upper, hidden) in zip(gates, uppers, downs, kept):
        g_downs.append(product_left(d_full, hidden).astype(half))
        _, pull = jax.vjp(gated, gate, upper)
        d_gate, d_upper = pull(product(d_full, w_down))
        d_gate = d_gate.astype(half)
        d_upper = d_upper.astype(half)
        g_gates.append(product_left(x_in, d_gate).astype(half))
        g_uppers.append(product_left(x_in, d_upper).astype(half))
        d_in = d_in + product_right(d_gate, w_gate) + product_right(d_upper, w_upper)
    return g_gates, g_uppers, g_downs, d_in


def adam(weight, grad, first, second, step_rate):
    first = beta_one * first + (1 - beta_one) * grad
    second = beta_two * second + (1 - beta_two) * grad * grad
    step_size = first / (1 - beta_one**STEP) / (jnp.sqrt(second / (1 - beta_two**STEP)) + adam_eps)
    return (weight - step_rate * (step_size + decay * weight), first, second)


def own_part(whole, rows):
    return lax.dynamic_slice_in_dim(whole, lax.axis_index("c") * rows, rows)


def positions(rows):
    core = lax.axis_index("c")
    near = jnp.arange(rows, dtype=jnp.int32)
    return jnp.concatenate([core * rows + near, (1 - core) * rows + near])


def on_device(axes, *args):
    source_ids, target_ids, source_lengths, target_lengths = args[:4]
    masters, firsts, seconds = args[4:11], args[11:18], args[18:25]
    embedding, unembedding, attention_in, attention_out, feed_in, feed_out, norm_gains = masters
    row = lax.axis_index("y")
    core = lax.axis_index("c")
    everywhere = axes + ("y", "c")

    vocab_rows = embedding.shape[0]
    table_pair = jnp.concatenate([embedding.T.astype(half), unembedding.astype(half)], axis=1)
    table_pairs = gather_unit(table_pair, axes, True)
    table_pairs = table_pairs + [spin(p, "c", 1) for p in table_pairs]
    table_t = jnp.concatenate([p[:, :vocab_rows] for p in table_pairs], axis=1)
    w_head = jnp.concatenate([p[:, vocab_rows:] for p in table_pairs], axis=1)
    near = jnp.arange(vocab_rows, dtype=jnp.int32)
    vocab_ids = jnp.concatenate(
        [
            ((row ^ y_step) * 2 + (core ^ c_step)) * vocab_rows + near
            for c_step in (0, 1)
            for y_step in (0, 1)
        ]
    )

    own_count = jnp.sum(target_lengths).astype(jnp.float32)
    gain_part = jnp.concatenate(
        [norm_gains, jnp.full((1, norm_gains.shape[1]), own_count, jnp.float32)]
    )
    gain_part = in_order(gain_part, spin(gain_part, "c", 1), "c")
    gain_part = in_order(gain_part, spin(gain_part, "y", 1), "y")
    feature_rows = gain_part.shape[1]
    gain_part = gain_part.T
    for axis in axes:
        gain_part = gather_rows(gain_part, axis)
    gains = gain_part.T
    count = jnp.sum(gain_part[::feature_rows, -1])
    gains = gains[:-1]

    def attention_unit(layer):
        w_in = attention_in[layer].astype(half)
        w_in = w_in.reshape(w_in.shape[0], -1)
        return jnp.concatenate([w_in, attention_out[layer].T.astype(half)], axis=1)

    def feed_units(layer):
        return (
            feed_in[layer, :, 0].astype(half),
            feed_in[layer, :, 1].astype(half),
            feed_out[layer].T.astype(half),
        )

    attn_order = (True, False, False)
    feed_order = ((True, False, True), (False, True, False))
    attn = [None] * 3
    feed = [None] * 2
    attn[0] = gather_unit(attention_unit(0), axes, attn_order[0])
    feed[0] = [gather_unit(u, axes, o) for u, o in zip(feed_units(0), feed_order[0])]
    attn[1] = gather_unit(attention_unit(1), axes, attn_order[1])
    attn[2] = gather_unit(attention_unit(2), axes, attn_order[2])
    feed[1] = [gather_unit(u, axes, o) for u, o in zip(feed_units(1), feed_order[1])]

    source = lax.dynamic_index_in_dim(source_ids, row, 0, False)[0]
    target = lax.dynamic_index_in_dim(target_ids, row, 0, False)[0]
    source_len = lax.dynamic_index_in_dim(source_lengths, row, 0, False)[0]
    target_len = lax.dynamic_index_in_dim(target_lengths, row, 0, False)[0]
    src_rows = source.shape[0] // 2
    tgt_rows = target.shape[0] // 2
    src_pos = positions(src_rows)
    tgt_pos = positions(tgt_rows)
    key_bias = jnp.where(src_pos < source_len, 0.0, masked)[None, None, :]
    causal = jnp.where(tgt_pos[:, None] >= tgt_pos[None, :], 0.0, masked)[None]
    shifted = jnp.concatenate([jnp.zeros((1,), jnp.int32), target[:-1]])
    source_hot = (own_part(source, src_rows)[:, None] == vocab_ids[None, :]).astype(half)
    target_hot = (own_part(shifted, tgt_rows)[:, None] == vocab_ids[None, :]).astype(half)
    hits = own_part(target, tgt_rows)[:, None] == vocab_ids[None, :]

    src_embed = product_right(source_hot, table_t)
    src_norm_a = collect(normalize(src_embed, gains[0]))
    part, keep_src_a = self_attention(src_norm_a, attn[0], key_bias)
    src_mid = src_embed + fold(part)
    src_norm_b = collect(normalize(src_mid, gains[1]))
    part, keep_src_b = expand(src_norm_b, *feed[0])
    src_top = src_mid + fold(part)
    encoded = collect(normalize(src_top, gains[2]))

    tgt_embed = product_right(target_hot, table_t)
    tgt_norm_a = collect(normalize(tgt_embed, gains[3]))
    part, keep_tgt_a = self_attention(tgt_norm_a, attn[1], causal)
    tgt_self = tgt_embed + fold(part)
    tgt_norm_b = collect(normalize(tgt_self, gains[4]))
    part, keep_tgt_b = cross_attention(tgt_norm_b, encoded, attn[2], key_bias)
    tgt_cross = tgt_self + fold(part)
    tgt_norm_c = collect(normalize(tgt_cross, gains[5]))
    part, keep_tgt_c = expand(tgt_norm_c, *feed[1])
    tgt_top = tgt_cross + fold(part)
    tgt_norm_d = normalize(tgt_top, gains[6])

    logits = product(tgt_norm_d, w_head)
    peak = jnp.max(logits, axis=-1, keepdims=True)
    lse = peak + jnp.log(jnp.sum(jnp.exp(logits - peak), axis=-1, keepdims=True))
    picked = jnp.sum(jnp.where(hits, logits, 0.0), axis=-1, keepdims=True)
    weight = (tgt_pos[:tgt_rows] < target_len).astype(jnp.float32)[:, None] / count
    own_loss = jnp.sum((lse - picked) * weight)
    d_logits = ((jnp.exp(logits - lse) - hits.astype(jnp.float32)) * weight).astype(half)
    g_head = product_left(tgt_norm_d, d_logits).astype(half)

    attn_grads = [None] * 3
    feed_grads = [None] * 2
    d_tgt, gain_six = norm_back(tgt_top, gains[6], product_right(d_logits, w_head))
    *grads, d_in = expand_back(tgt_norm_c, *feed[1], keep_tgt_c, collect(d_tgt.astype(half)))
    feed_grads[1] = [scatter_unit(g, axes, o) for g, o in zip(grads, feed_order[1])]
    d_more, gain_five = norm_back(tgt_cross, gains[5], fold(d_in))
    d_tgt = d_tgt + d_more
    grads, d_query, d_keys = cross_attention_back(
        tgt_norm_b, encoded, attn[2], key_bias, keep_tgt_b, collect(d_tgt.astype(half))
    )
    attn_grads[2] = scatter_unit(grads, axes, attn_order[2])
    d_encoded = fold(d_keys)
    d_more, gain_four = norm_back(tgt_self, gains[4], fold(d_query))
    d_tgt = d_tgt + d_more
    grads, d_in = self_attention_back(
        tgt_norm_a, attn[1], causal, keep_tgt_a, collect(d_tgt.astype(half))
    )
    attn_grads[1] = scatter_unit(grads, axes, attn_order[1])
    d_more, gain_three = norm_back(tgt_embed, gains[3], fold(d_in))
    d_tgt = d_tgt + d_more

    d_src, gain_two = norm_back(src_top, gains[2], d_encoded)
    *grads, d_in = expand_back(src_norm_b, *feed[0], keep_src_b, collect(d_src.astype(half)))
    feed_grads[0] = [scatter_unit(g, axes, o) for g, o in zip(grads, feed_order[0])]
    d_more, gain_one = norm_back(src_mid, gains[1], fold(d_in))
    d_src = d_src + d_more
    grads, d_in = self_attention_back(
        src_norm_a, attn[0], key_bias, keep_src_a, collect(d_src.astype(half))
    )
    attn_grads[0] = scatter_unit(grads, axes, attn_order[0])
    d_more, gain_zero = norm_back(src_embed, gains[0], fold(d_in))
    d_src = d_src + d_more

    g_table = product_left(d_src.astype(half), source_hot)
    g_table = (g_table + product_left(d_tgt.astype(half), target_hot)).astype(half)
    pairs = [
        jnp.concatenate(
            [
                g_table[:, k * vocab_rows : (k + 1) * vocab_rows],
                g_head[:, k * vocab_rows : (k + 1) * vocab_rows],
            ],
            axis=1,
        )
        for k in range(4)
    ]
    pairs = [
        (a.astype(jnp.float32) + spin(b, "c", 1).astype(jnp.float32)).astype(half)
        for a, b in zip(pairs[:2], pairs[2:])
    ]
    pair_grad = scatter_unit(pairs, axes, True)

    g_gains = jnp.stack([gain_zero, gain_one, gain_two, gain_three, gain_four, gain_five, gain_six])
    g_gains = g_gains.T
    for axis in axes[::-1]:
        g_gains = scatter_rows(g_gains, axis)
    g_gains = total_over(g_gains, ("y", "c"))
    own_gains = norm_gains.shape[1]
    g_gains = lax.dynamic_slice_in_dim(g_gains, (row * 2 + core) * own_gains, own_gains).T

    width = attention_out.shape[1]
    units = [pair_grad] + attn_grads + feed_grads[0] + feed_grads[1]
    squares = sum(jnp.sum(g * g) for g in units) + jnp.sum(g_gains * g_gains)
    squares, loss = total_over(jnp.stack([squares, own_loss]), everywhere)
    grads = (
        pair_grad[:, :vocab_rows].T,
        pair_grad[:, vocab_rows:],
        jnp.stack([g[:, : 3 * width].reshape(-1, 3, width) for g in attn_grads]),
        jnp.stack([g[:, 3 * width :].T for g in attn_grads]),
        jnp.stack([jnp.stack([g[0], g[1]], axis=1) for g in feed_grads]),
        jnp.stack([g[2].T for g in feed_grads]),
        g_gains,
    )
    grad_norm = jnp.sqrt(squares)
    scale = jnp.minimum(1.0, clip_limit / grad_norm)
    results = [
        adam(w, g * scale, m, v, r)
        for w, g, m, v, r in zip(masters, grads, firsts, seconds, step_rates)
    ]
    return (loss, grad_norm) + tuple(r[i] for i in range(3) for r in results)


def solution(mesh):
    data = mesh.shape["dp"]
    sizes = [2]
    data //= 2
    while data > 1:
        size = 4 if data % 4 == 0 else data
        sizes.insert(0, size)
        data //= size
    axes = tuple(f"d{i}" for i in range(len(sizes)))
    devices = np.asarray(mesh.devices).reshape(tuple(sizes) + (mesh.shape["mp"] // 2, 2))
    inner = Mesh(devices, axes + ("y", "c"))
    dp = axes
    mp = ("y", "c")
    params = (
        P(mp, dp),
        P(dp, mp),
        P(None, dp, None, mp),
        P(None, mp, dp),
        P(None, dp, None, mp),
        P(None, mp, dp),
        P(None, dp + mp),
    )
    ids = (P(None, dp, None), P(None, dp, None), P(None, dp), P(None, dp))
    return jax.shard_map(
        lambda *args: on_device(axes, *args),
        mesh=inner,
        in_specs=ids + params * 3,
        out_specs=(P(), P()) + params * 3,
        check_vma=False,
    )
```

```python
import jax
import jax.numpy as jnp
import numpy as np
from jax import lax
from jax.experimental.layout import Layout, with_layout_constraint
from jax.sharding import Mesh
from jax.sharding import PartitionSpec as P

DK = 64
STEP = 10


norm_eps = 1e-06
clip_limit = 0.05
step_rates = (0.4, 0.02, 0.02, 0.1, 0.02, 0.02, 0.25)
beta_one = 0.9
beta_two = 0.999
adam_eps = 1e-08
decay = 0.01
masked = -1000000000.0

half = jnp.bfloat16


def spin(part, axis, shift):
    size = lax.axis_size(axis)
    return lax.ppermute(part, axis, [(i, (i + shift) % size) for i in range(size)])


def flip(part, axis, bit):
    size = lax.axis_size(axis)
    return lax.ppermute(part, axis, [(i, i ^ bit) for i in range(size)])


def plain(part):
    return with_layout_constraint(part, Layout(major_to_minor=tuple(range(part.ndim))))


def gather_unit(part):
    whole = lax.all_gather(plain(part), ("y", "dp"), axis=0, tiled=True)
    rows = whole.shape[0] // 2
    return [whole[:rows], whole[rows:]]


def scatter_unit(parts):
    whole = plain(jnp.concatenate(parts, axis=0))
    part = lax.psum_scatter(whole, ("y", "dp"), scatter_dimension=0, tiled=True)
    return part.astype(jnp.float32)


def join_step(part, place, axis, bit):
    other = flip(part, axis, bit)
    mine = (lax.axis_index(axis) // bit) % 2 == 0
    return jnp.stack([jnp.where(mine, part, other), jnp.where(mine, other, part)], axis=place)


def gather_pairs(part, row_first):
    bits = (lax.axis_size("dp") - 1).bit_length()
    part = plain(part)
    for bit in range(bits - 1, 0, -1):
        part = join_step(part, bits - 1 - bit, "dp", 1 << bit)
    if row_first:
        part = join_step(part, 0, "y", 1)
        part = join_step(part, bits, "dp", 1)
    else:
        part = join_step(part, bits - 1, "dp", 1)
        part = join_step(part, 0, "y", 1)
    part = part.reshape(2, -1, part.shape[-1])
    return [part[0], part[1]]


def split_step(whole, place, axis, bit):
    mine = (lax.axis_index(axis) // bit) % 2
    own = lax.dynamic_index_in_dim(whole, mine, place, False)
    sent = lax.dynamic_index_in_dim(whole, 1 - mine, place, False)
    return own.astype(jnp.float32) + flip(sent, axis, bit).astype(jnp.float32)


def scatter_pairs(parts, row_first):
    bits = (lax.axis_size("dp") - 1).bit_length()
    whole = jnp.stack([plain(p) for p in parts])
    columns = whole.shape[2]
    whole = whole.reshape((2,) + (2,) * bits + (-1, columns))
    if row_first:
        whole = split_step(whole, 0, "y", 1).astype(half)
        whole = split_step(whole, bits - 1, "dp", 1)
    else:
        whole = split_step(whole, bits, "dp", 1).astype(half)
        whole = split_step(whole, 0, "y", 1)
    for bit in range(1, bits):
        whole = split_step(whole.astype(half), bits - 1 - bit, "dp", 1 << bit)
    return whole


def total_over(value, axes):
    for axis in axes:
        bit = 1
        while bit < lax.axis_size(axis):
            value = value + flip(value, axis, bit)
            bit *= 2
    return value


def collect(own):
    return jnp.concatenate([own, spin(own, "c", 1)], axis=0)


def fold(part):
    rows = part.shape[0] // 2
    return part[:rows] + spin(part[rows:].astype(half), "c", 1).astype(jnp.float32)


def product(left, right):
    return jnp.dot(left, right, preferred_element_type=jnp.float32)


def product_left(left, right):
    return lax.dot_general(
        left, right, (((0,), (0,)), ((), ())), preferred_element_type=jnp.float32
    )


def product_right(left, right):
    return lax.dot_general(
        left, right, (((1,), (1,)), ((), ())), preferred_element_type=jnp.float32
    )


def rms_norm(stream, gain):
    return stream * lax.rsqrt(jnp.mean(stream * stream, axis=-1, keepdims=True) + norm_eps) * gain


def normalize(stream, gain):
    return rms_norm(stream, gain).astype(half)


def norm_back(stream, gain, grad):
    _, pull = jax.vjp(rms_norm, stream, gain)
    return pull(grad)


def heads(flat):
    return flat.reshape(flat.shape[0], -1, DK)


def score_block(query, key, bias):
    return (
        jnp.einsum("rhd,shd->hrs", heads(query), heads(key), preferred_element_type=jnp.float32)
        * 0.125
        + bias
    )


def attend(query, key, value, bias):
    scores = score_block(query, key, bias)
    peak = jnp.max(scores, axis=-1, keepdims=True)
    raw = jnp.exp(scores - peak)
    total = jnp.sum(raw, axis=-1, keepdims=True)
    probs = (raw / total).astype(half)
    mixed = jnp.einsum("hrs,shd->rhd", probs, heads(value), preferred_element_type=jnp.float32)
    mixed = mixed.reshape(query.shape[0], -1).astype(half)
    return mixed, peak + jnp.log(total)


def attend_back(query, key, value, lse, bias, d_mixed):
    rows = query.shape[0]
    cols = key.shape[0]
    d_heads = heads(d_mixed)
    probs = jnp.exp(score_block(query, key, bias) - lse)
    d_value = jnp.einsum(
        "hrs,rhd->shd", probs.astype(half), d_heads, preferred_element_type=jnp.float32
    )
    d_probs = jnp.einsum("rhd,shd->hrs", d_heads, heads(value), preferred_element_type=jnp.float32)
    d_scores = (probs * (d_probs - jnp.sum(probs * d_probs, axis=-1, keepdims=True))).astype(half)
    d_query = (
        jnp.einsum("hrs,shd->rhd", d_scores, heads(key), preferred_element_type=jnp.float32) * 0.125
    )
    d_key = (
        jnp.einsum("hrs,rhd->shd", d_scores, heads(query), preferred_element_type=jnp.float32)
        * 0.125
    )
    return (
        d_query.reshape(rows, -1).astype(half),
        d_key.reshape(cols, -1).astype(half),
        d_value.reshape(cols, -1).astype(half),
    )


def self_attention(x_in, blocks, bias):
    part = 0.0
    kept = []
    for block in blocks:
        width = block.shape[1] // 4
        qkv = product(x_in, block[:, : 3 * width]).astype(half)
        query, key, value = qkv[:, :width], qkv[:, width : 2 * width], qkv[:, 2 * width :]
        mixed, lse = attend(query, key, value, bias)
        part = part + product_right(mixed, block[:, 3 * width :])
        kept.append((query, key, value, lse, mixed))
    return part, kept


def self_attention_back(x_in, blocks, bias, kept, d_full):
    d_in = 0.0
    grads = []
    for block, (query, key, value, lse, mixed) in zip(blocks, kept):
        width = block.shape[1] // 4
        g_out = product_left(d_full, mixed).astype(half)
        d_mixed = product(d_full, block[:, 3 * width :]).astype(half)
        d_qkv = jnp.concatenate(attend_back(query, key, value, lse, bias, d_mixed), axis=1)
        g_in = product_left(x_in, d_qkv).astype(half)
        grads.append(jnp.concatenate([g_in, g_out], axis=1))
        d_in = d_in + product_right(d_qkv, block[:, : 3 * width])
    return grads, d_in


def cross_attention(x_in, x_keys, blocks, bias):
    part = 0.0
    kept = []
    for block in blocks:
        width = block.shape[1] // 4
        query = product(x_in, block[:, :width]).astype(half)
        pair = product(x_keys, block[:, width : 3 * width]).astype(half)
        key, value = pair[:, :width], pair[:, width:]
        mixed, lse = attend(query, key, value, bias)
        part = part + product_right(mixed, block[:, 3 * width :])
        kept.append((query, key, value, lse, mixed))
    return part, kept


def cross_attention_back(x_in, x_keys, blocks, bias, kept, d_full):
    d_in = 0.0
    d_keys = 0.0
    grads = []
    for block, (query, key, value, lse, mixed) in zip(blocks, kept):
        width = block.shape[1] // 4
        g_out = product_left(d_full, mixed).astype(half)
        d_mixed = product(d_full, block[:, 3 * width :]).astype(half)
        d_query, d_key, d_value = attend_back(query, key, value, lse, bias, d_mixed)
        d_pair = jnp.concatenate([d_key, d_value], axis=1)
        g_query = product_left(x_in, d_query).astype(half)
        g_pair = product_left(x_keys, d_pair).astype(half)
        grads.append(jnp.concatenate([g_query, g_pair, g_out], axis=1))
        d_in = d_in + product_right(d_query, block[:, :width])
        d_keys = d_keys + product_right(d_pair, block[:, width : 3 * width])
    return grads, d_in, d_keys


def gated(gate, upper):
    return jax.nn.gelu(gate, approximate=True) * upper


def expand(x_in, gates, uppers, downs):
    part = 0.0
    kept = []
    for w_gate, w_upper, w_down in zip(gates, uppers, downs):
        gate = product(x_in, w_gate)
        upper = product(x_in, w_upper)
        hidden = gated(gate, upper).astype(half)
        part = part + product_right(hidden, w_down)
        kept.append((gate, upper, hidden))
    return part, kept


def expand_back(x_in, gates, uppers, downs, kept, d_full):
    d_in = 0.0
    g_gates, g_uppers, g_downs = [], [], []
    for w_gate, w_upper, w_down, (gate, upper, hidden) in zip(gates, uppers, downs, kept):
        g_downs.append(product_left(d_full, hidden).astype(half))
        _, pull = jax.vjp(gated, gate, upper)
        d_gate, d_upper = pull(product(d_full, w_down))
        d_gate = d_gate.astype(half)
        d_upper = d_upper.astype(half)
        g_gates.append(product_left(x_in, d_gate).astype(half))
        g_uppers.append(product_left(x_in, d_upper).astype(half))
        d_in = d_in + product_right(d_gate, w_gate) + product_right(d_upper, w_upper)
    return g_gates, g_uppers, g_downs, d_in


def adam(weight, grad, first, second, step_rate):
    first = beta_one * first + (1 - beta_one) * grad
    second = beta_two * second + (1 - beta_two) * grad * grad
    step_size = first / (1 - beta_one**STEP) / (jnp.sqrt(second / (1 - beta_two**STEP)) + adam_eps)
    return (weight - step_rate * (step_size + decay * weight), first, second)


def own_part(whole, rows):
    return lax.dynamic_slice_in_dim(whole, lax.axis_index("c") * rows, rows)


def positions(rows):
    core = lax.axis_index("c")
    near = jnp.arange(rows, dtype=jnp.int32)
    return jnp.concatenate([core * rows + near, (1 - core) * rows + near])


def on_device(*args):
    source_ids, target_ids, source_lengths, target_lengths = args[:4]
    masters, firsts, seconds = args[4:11], args[11:18], args[18:25]
    embedding, unembedding, attention_in, attention_out, feed_in, feed_out, norm_gains = masters
    row = lax.axis_index("y")
    core = lax.axis_index("c")
    everywhere = ("dp", "y", "c")
    size = lax.axis_size("dp")

    vocab_rows = embedding.shape[0]
    table_pair = jnp.concatenate([embedding.T.astype(half), unembedding.astype(half)], axis=1)
    vocab_ids = jnp.arange(4 * vocab_rows, dtype=jnp.int32)

    own_count = jnp.sum(target_lengths).astype(jnp.float32)
    gain_part = jnp.concatenate(
        [norm_gains, jnp.full((1, norm_gains.shape[1]), own_count, jnp.float32)]
    )
    gain_part = lax.all_gather(gain_part, everywhere)
    count = jnp.sum(gain_part[::4, -1, 0])
    gains = gain_part[:, :-1].swapaxes(0, 1).reshape(norm_gains.shape[0], -1)

    hidden_rows = feed_out.shape[1]
    spare = ((0, 0), (0, -hidden_rows % 128))

    def attention_unit(layer):
        w_in = attention_in[layer].astype(half)
        w_in = w_in.reshape(w_in.shape[0], -1)
        return [w_in, attention_out[layer].T.astype(half)]

    def feed_units(layer):
        return [
            jnp.pad(feed_in[layer, :, 0].astype(half), spare),
            jnp.pad(feed_in[layer, :, 1].astype(half), spare),
            jnp.pad(feed_out[layer].T.astype(half), spare),
        ]

    def thirds(blocks, start):
        third = hidden_rows + spare[1][1]
        return [
            [b[:, start + k * third : start + (k + 1) * third] for b in blocks] for k in range(3)
        ]

    first = gather_unit(jnp.concatenate(attention_unit(0) + feed_units(0) + [table_pair], axis=1))
    second = gather_unit(jnp.concatenate(feed_units(1), axis=1))
    span = 4 * attention_out.shape[1]
    edge = first[0].shape[1] - 2 * vocab_rows
    attn = (
        [b[:, :span] for b in first],
        gather_pairs(jnp.concatenate(attention_unit(1), axis=1), False),
        gather_pairs(jnp.concatenate(attention_unit(2), axis=1), True),
    )
    feed = (thirds(first, span), thirds(second, 0))
    table_pairs = join_step(jnp.stack([plain(b[:, edge:]) for b in first]), 1, "c", 1)
    table_pairs = table_pairs.reshape(4, -1, 2, vocab_rows).transpose(2, 1, 0, 3)
    table_t, w_head = table_pairs.reshape(2, -1, 4 * vocab_rows)

    source = lax.dynamic_index_in_dim(source_ids, row, 0, False)[0]
    target = lax.dynamic_index_in_dim(target_ids, row, 0, False)[0]
    source_len = lax.dynamic_index_in_dim(source_lengths, row, 0, False)[0]
    target_len = lax.dynamic_index_in_dim(target_lengths, row, 0, False)[0]
    src_rows = source.shape[0] // 2
    tgt_rows = target.shape[0] // 2
    src_pos = positions(src_rows)
    tgt_pos = positions(tgt_rows)
    key_bias = jnp.where(src_pos < source_len, 0.0, masked)[None, None, :]
    causal = jnp.where(tgt_pos[:, None] >= tgt_pos[None, :], 0.0, masked)[None]
    shifted = jnp.concatenate([jnp.zeros((1,), jnp.int32), target[:-1]])
    source_hot = (own_part(source, src_rows)[:, None] == vocab_ids[None, :]).astype(half)
    target_hot = (own_part(shifted, tgt_rows)[:, None] == vocab_ids[None, :]).astype(half)
    hits = own_part(target, tgt_rows)[:, None] == vocab_ids[None, :]

    src_embed = product_right(source_hot, table_t)
    src_norm_a = collect(normalize(src_embed, gains[0]))
    part, keep_src_a = self_attention(src_norm_a, attn[0], key_bias)
    src_mid = src_embed + fold(part)
    src_norm_b = collect(normalize(src_mid, gains[1]))
    part, keep_src_b = expand(src_norm_b, *feed[0])
    src_top = src_mid + fold(part)
    encoded = collect(normalize(src_top, gains[2]))

    tgt_embed = product_right(target_hot, table_t)
    tgt_norm_a = collect(normalize(tgt_embed, gains[3]))
    part, keep_tgt_a = self_attention(tgt_norm_a, attn[1], causal)
    tgt_self = tgt_embed + fold(part)
    tgt_norm_b = collect(normalize(tgt_self, gains[4]))
    part, keep_tgt_b = cross_attention(tgt_norm_b, encoded, attn[2], key_bias)
    tgt_cross = tgt_self + fold(part)
    tgt_norm_c = collect(normalize(tgt_cross, gains[5]))
    part, keep_tgt_c = expand(tgt_norm_c, *feed[1])
    tgt_top = tgt_cross + fold(part)
    tgt_norm_d = normalize(tgt_top, gains[6])

    logits = product(tgt_norm_d, w_head)
    peak = jnp.max(logits, axis=-1, keepdims=True)
    lse = peak + jnp.log(jnp.sum(jnp.exp(logits - peak), axis=-1, keepdims=True))
    picked = jnp.sum(jnp.where(hits, logits, 0.0), axis=-1, keepdims=True)
    weight = (tgt_pos[:tgt_rows] < target_len).astype(jnp.float32)[:, None] / count
    own_loss = jnp.sum((lse - picked) * weight)
    d_logits = ((jnp.exp(logits - lse) - hits.astype(jnp.float32)) * weight).astype(half)
    g_head = product_left(tgt_norm_d, d_logits).astype(half)

    d_tgt, gain_six = norm_back(tgt_top, gains[6], product_right(d_logits, w_head))
    *feed_one, d_in = expand_back(tgt_norm_c, *feed[1], keep_tgt_c, collect(d_tgt.astype(half)))
    *feed_one, down_one = feed_one
    down_one = scatter_pairs(down_one, False)
    feed_one = scatter_unit([jnp.concatenate([plain(p) for p in g], axis=1) for g in zip(*feed_one)])
    d_more, gain_five = norm_back(tgt_cross, gains[5], fold(d_in))
    d_tgt = d_tgt + d_more
    attn_two, d_query, d_keys = cross_attention_back(
        tgt_norm_b, encoded, attn[2], key_bias, keep_tgt_b, collect(d_tgt.astype(half))
    )
    attn_two = scatter_pairs(attn_two, True)
    d_encoded = fold(d_keys)
    d_more, gain_four = norm_back(tgt_self, gains[4], fold(d_query))
    d_tgt = d_tgt + d_more
    attn_one, d_in = self_attention_back(
        tgt_norm_a, attn[1], causal, keep_tgt_a, collect(d_tgt.astype(half))
    )
    attn_one = scatter_pairs(attn_one, False)
    d_more, gain_three = norm_back(tgt_embed, gains[3], fold(d_in))
    d_tgt = d_tgt + d_more

    d_src, gain_two = norm_back(src_top, gains[2], d_encoded)
    *feed_zero, d_in = expand_back(src_norm_b, *feed[0], keep_src_b, collect(d_src.astype(half)))
    *feed_zero, down_zero = feed_zero
    down_zero = scatter_pairs(down_zero, False)
    feed_zero = scatter_unit(
        [jnp.concatenate([plain(p) for p in g], axis=1) for g in zip(*feed_zero)]
    )
    d_more, gain_one = norm_back(src_mid, gains[1], fold(d_in))
    d_src = d_src + d_more
    attn_zero, d_in = self_attention_back(
        src_norm_a, attn[0], key_bias, keep_src_a, collect(d_src.astype(half))
    )
    attn_zero = scatter_pairs(attn_zero, True)
    d_more, gain_zero = norm_back(src_embed, gains[0], fold(d_in))
    d_src = d_src + d_more

    g_table = product_left(d_src.astype(half), source_hot)
    g_table = (g_table + product_left(d_tgt.astype(half), target_hot)).astype(half)
    pairs = jnp.stack([g_table, g_head], axis=1).reshape(-1, 2, 2, 2, vocab_rows)
    pairs = pairs.transpose(2, 3, 0, 1, 4).reshape(2, 2, -1, 2 * vocab_rows)
    pairs = split_step(pairs, 1, "c", 1).astype(half)
    pair_grad = scatter_pairs([pairs[0], pairs[1]], False)

    g_gains = jnp.stack([gain_zero, gain_one, gain_two, gain_three, gain_four, gain_five, gain_six])
    g_gains = g_gains.T.reshape((2,) * (size - 1).bit_length() + (2, 2, -1, g_gains.shape[0]))
    for axis in ("c", "y"):
        g_gains = split_step(g_gains, g_gains.ndim - 3, axis, 1)
    for bit in range((size - 1).bit_length()):
        g_gains = split_step(g_gains, g_gains.ndim - 3, "dp", 1 << bit)
    g_gains = g_gains.T

    width = attention_out.shape[1]
    attn_grads = [attn_zero, attn_one, attn_two]
    units = [pair_grad, *attn_grads, feed_zero, feed_one, down_zero, down_one]
    squares = sum(jnp.sum(g * g) for g in units) + jnp.sum(g_gains * g_gains)
    feed_grads = [g.reshape(-1, 2, hidden_rows + spare[1][1]) for g in (feed_zero, feed_one)]
    squares, loss = total_over(jnp.stack([squares, own_loss]), everywhere)
    grads = (
        pair_grad[:, :vocab_rows].T,
        pair_grad[:, vocab_rows:],
        jnp.stack([g[:, : 3 * width].reshape(-1, 3, width) for g in attn_grads]),
        jnp.stack([g[:, 3 * width :].T for g in attn_grads]),
        jnp.stack(feed_grads)[..., :hidden_rows],
        jnp.stack([g.T[:hidden_rows] for g in (down_zero, down_one)]),
        g_gains,
    )
    grads = tuple(plain(g) for g in grads)
    grad_norm = jnp.sqrt(squares)
    scale = jnp.minimum(1.0, clip_limit / grad_norm)
    results = [
        adam(w, g * scale, m, v, r)
        for w, g, m, v, r in zip(masters, grads, firsts, seconds, step_rates)
    ]
    return (loss, grad_norm) + tuple(r[i] for i in range(3) for r in results)


def solution(mesh):
    shape = (mesh.shape["dp"], mesh.shape["mp"] // 2, 2)
    inner = Mesh(np.asarray(mesh.devices).reshape(shape), ("dp", "y", "c"))
    dp = "dp"
    mp = ("y", "c")
    params = (
        P(mp, dp),
        P(dp, mp),
        P(None, dp, None, mp),
        P(None, mp, dp),
        P(None, dp, None, mp),
        P(None, mp, dp),
        P(None, (dp,) + mp),
    )
    ids = (P(None, dp, None), P(None, dp, None), P(None, dp), P(None, dp))
    return jax.shard_map(
        on_device,
        mesh=inner,
        in_specs=ids + params * 3,
        out_specs=(P(), P()) + params * 3,
        check_vma=False,
    )
```

```python
import jax
import jax.numpy as jnp
import numpy as np
from jax import lax
from jax.experimental.layout import Layout, with_layout_constraint
from jax.sharding import Mesh
from jax.sharding import PartitionSpec as P

DK = 64
STEP = 10


norm_eps = 1e-06
clip_limit = 0.05
step_rates = (0.4, 0.02, 0.02, 0.1, 0.02, 0.02, 0.25)
beta_one = 0.9
beta_two = 0.999
adam_eps = 1e-08
decay = 0.01
masked = -1000000000.0

half = jnp.bfloat16


def spin(part, axis, shift):
    size = lax.axis_size(axis)
    return lax.ppermute(part, axis, [(i, (i + shift) % size) for i in range(size)])


def flip(part, axis, bit):
    size = lax.axis_size(axis)
    return lax.ppermute(part, axis, [(i, i ^ bit) for i in range(size)])


def plain(part):
    return with_layout_constraint(part, Layout(major_to_minor=tuple(range(part.ndim))))


def ordered(part, order):
    return with_layout_constraint(part, Layout(major_to_minor=order))


def gather_unit(part):
    whole = lax.all_gather(plain(part), ("y", "near", "far"), axis=0, tiled=True)
    rows = whole.shape[0] // 2
    return [whole[:rows], whole[rows:]]


def scatter_unit(blocks):
    rows, columns = blocks[0][0].shape
    whole = jnp.zeros((2 * rows, len(blocks) * columns), half)
    for k, pair in enumerate(blocks):
        for y, part in enumerate(pair):
            whole = lax.dynamic_update_slice(whole, plain(part), (y * rows, k * columns))
    part = lax.psum_scatter(
        plain(whole), ("y", "near", "far"), scatter_dimension=0, tiled=True
    )
    return part.astype(jnp.float32)


def choose(parts, axis):
    first = lax.axis_index(axis) == 0
    own = jnp.where(first, parts[0], parts[1]).astype(jnp.float32)
    sent = plain(jnp.where(first, parts[1], parts[0]))
    return own + flip(sent, axis, 1).astype(jnp.float32)


def split_rows(whole, axis, bit):
    rows = whole.shape[0] // 2
    mine = (lax.axis_index(axis) // bit) % 2
    own = lax.dynamic_slice_in_dim(whole, mine * rows, rows)
    sent = plain(lax.dynamic_slice_in_dim(whole, (1 - mine) * rows, rows))
    return own.astype(jnp.float32) + flip(sent, axis, bit).astype(jnp.float32)


def scatter_rows(part, kind):
    part = split_rows(part.astype(kind), "near", 1)
    bit = lax.axis_size("far") // 2
    while bit:
        part = split_rows(part.astype(kind), "far", bit)
        bit //= 2
    return part


def scatter_pairs(parts):
    return scatter_rows(choose([plain(p) for p in parts], "y"), half)


def total_over(value, axes):
    for axis in axes:
        bit = 1
        while bit < lax.axis_size(axis):
            value = value + flip(value, axis, bit)
            bit *= 2
    return value


def collect(own):
    return jnp.concatenate([own, spin(own, "c", 1)], axis=0)


def fold(part):
    rows = part.shape[0] // 2
    return part[:rows] + spin(part[rows:].astype(half), "c", 1).astype(jnp.float32)


def product(left, right):
    return jnp.dot(left, right, preferred_element_type=jnp.float32)


def product_left(left, right):
    return lax.dot_general(
        left, right, (((0,), (0,)), ((), ())), preferred_element_type=jnp.float32
    )


def product_right(left, right):
    return lax.dot_general(
        left, right, (((1,), (1,)), ((), ())), preferred_element_type=jnp.float32
    )


def rms_norm(stream, gain):
    return stream * lax.rsqrt(jnp.mean(stream * stream, axis=-1, keepdims=True) + norm_eps) * gain


def normalize(stream, gain):
    return rms_norm(stream, gain).astype(half)


def norm_back(stream, gain, grad):
    _, pull = jax.vjp(rms_norm, stream, gain)
    return pull(grad)


def heads(flat):
    return flat.reshape(flat.shape[0], -1, DK)


def score_block(query, key, bias):
    return (
        jnp.einsum("rhd,shd->hrs", heads(query), heads(key), preferred_element_type=jnp.float32)
        * 0.125
        + bias
    )


def attend(query, key, value, bias):
    scores = score_block(query, key, bias)
    peak = jnp.max(scores, axis=-1, keepdims=True)
    raw = jnp.exp(scores - peak)
    total = jnp.sum(raw, axis=-1, keepdims=True)
    probs = (raw / total).astype(half)
    mixed = jnp.einsum("hrs,shd->rhd", probs, heads(value), preferred_element_type=jnp.float32)
    mixed = mixed.reshape(query.shape[0], -1).astype(half)
    return mixed, peak + jnp.log(total)


def attend_back(query, key, value, lse, bias, d_mixed):
    rows = query.shape[0]
    cols = key.shape[0]
    d_heads = heads(d_mixed)
    probs = jnp.exp(score_block(query, key, bias) - lse)
    d_value = jnp.einsum(
        "hrs,rhd->shd", probs.astype(half), d_heads, preferred_element_type=jnp.float32
    )
    d_probs = jnp.einsum("rhd,shd->hrs", d_heads, heads(value), preferred_element_type=jnp.float32)
    d_scores = (probs * (d_probs - jnp.sum(probs * d_probs, axis=-1, keepdims=True))).astype(half)
    d_query = (
        jnp.einsum("hrs,shd->rhd", d_scores, heads(key), preferred_element_type=jnp.float32) * 0.125
    )
    d_key = (
        jnp.einsum("hrs,rhd->shd", d_scores, heads(query), preferred_element_type=jnp.float32)
        * 0.125
    )
    return (
        d_query.reshape(rows, -1).astype(half),
        d_key.reshape(cols, -1).astype(half),
        d_value.reshape(cols, -1).astype(half),
    )


def self_attention(x_in, blocks, bias):
    part = 0.0
    kept = []
    for block in blocks:
        width = block.shape[1] // 4
        qkv = product(x_in, block[:, : 3 * width]).astype(half)
        query, key, value = qkv[:, :width], qkv[:, width : 2 * width], qkv[:, 2 * width :]
        mixed, lse = attend(query, key, value, bias)
        part = part + product_right(mixed, block[:, 3 * width :])
        kept.append((query, key, value, lse, mixed))
    return part, kept


def self_attention_back(x_in, blocks, bias, kept, d_full):
    d_in = 0.0
    grads = []
    for block, (query, key, value, lse, mixed) in zip(blocks, kept):
        width = block.shape[1] // 4
        g_out = product_left(d_full, mixed).astype(half)
        d_mixed = product(d_full, block[:, 3 * width :]).astype(half)
        d_qkv = jnp.concatenate(attend_back(query, key, value, lse, bias, d_mixed), axis=1)
        g_in = product_left(x_in, d_qkv).astype(half)
        grads.append(jnp.concatenate([g_in, g_out], axis=1))
        d_in = d_in + product_right(d_qkv, block[:, : 3 * width])
    return grads, d_in


def cross_attention(x_in, x_keys, blocks, bias):
    part = 0.0
    kept = []
    for block in blocks:
        width = block.shape[1] // 4
        query = product(x_in, block[:, :width]).astype(half)
        pair = product(x_keys, block[:, width : 3 * width]).astype(half)
        key, value = pair[:, :width], pair[:, width:]
        mixed, lse = attend(query, key, value, bias)
        part = part + product_right(mixed, block[:, 3 * width :])
        kept.append((query, key, value, lse, mixed))
    return part, kept


def cross_attention_back(x_in, x_keys, blocks, bias, kept, d_full):
    d_in = 0.0
    d_keys = 0.0
    grads = []
    for block, (query, key, value, lse, mixed) in zip(blocks, kept):
        width = block.shape[1] // 4
        g_out = product_left(d_full, mixed).astype(half)
        d_mixed = product(d_full, block[:, 3 * width :]).astype(half)
        d_query, d_key, d_value = attend_back(query, key, value, lse, bias, d_mixed)
        d_pair = jnp.concatenate([d_key, d_value], axis=1)
        g_query = product_left(x_in, d_query).astype(half)
        g_pair = product_left(x_keys, d_pair).astype(half)
        grads.append(jnp.concatenate([g_query, g_pair, g_out], axis=1))
        d_in = d_in + product_right(d_query, block[:, :width])
        d_keys = d_keys + product_right(d_pair, block[:, width : 3 * width])
    return grads, d_in, d_keys


def gated(gate, upper):
    return jax.nn.gelu(gate, approximate=True) * upper


def expand(x_in, gates, uppers, downs):
    part = 0.0
    kept = []
    for w_gate, w_upper, w_down in zip(gates, uppers, downs):
        gate = product(x_in, w_gate)
        upper = product(x_in, w_upper)
        hidden = gated(gate, upper).astype(half)
        part = part + product_right(hidden, w_down)
        kept.append((gate, upper, hidden))
    return part, kept


def expand_back(x_in, gates, uppers, downs, kept, d_full):
    d_in = 0.0
    g_gates, g_uppers, g_downs = [], [], []
    for w_gate, w_upper, w_down, (gate, upper, hidden) in zip(gates, uppers, downs, kept):
        g_downs.append(product_left(d_full, hidden).astype(half))
        _, pull = jax.vjp(gated, gate, upper)
        d_gate, d_upper = pull(product(d_full, w_down))
        d_gate = d_gate.astype(half)
        d_upper = d_upper.astype(half)
        g_gates.append(product_left(x_in, d_gate).astype(half))
        g_uppers.append(product_left(x_in, d_upper).astype(half))
        d_in = d_in + product_right(d_gate, w_gate) + product_right(d_upper, w_upper)
    return g_gates, g_uppers, g_downs, d_in


def adam(weight, grad, first, second, step_rate):
    first = beta_one * first + (1 - beta_one) * grad
    second = beta_two * second + (1 - beta_two) * grad * grad
    step_size = first / (1 - beta_one**STEP) / (jnp.sqrt(second / (1 - beta_two**STEP)) + adam_eps)
    return (weight - step_rate * (step_size + decay * weight), first, second)


def own_part(whole, rows):
    return lax.dynamic_slice_in_dim(whole, lax.axis_index("c") * rows, rows)


def positions(rows):
    core = lax.axis_index("c")
    near = jnp.arange(rows, dtype=jnp.int32)
    return jnp.concatenate([core * rows + near, (1 - core) * rows + near])


def on_device(*args):
    source_ids, target_ids, source_lengths, target_lengths = args[:4]
    masters, firsts, seconds = args[4:11], args[11:18], args[18:25]
    embedding, unembedding, attention_in, attention_out, feed_in, feed_out, norm_gains = masters
    row = lax.axis_index("y")
    core = lax.axis_index("c")
    everywhere = ("near", "far", "y", "c")

    vocab_rows = embedding.shape[0]
    table_pair = jnp.concatenate([embedding.T.astype(half), unembedding.astype(half)], axis=1)
    near = jnp.arange(vocab_rows, dtype=jnp.int32)
    vocab_ids = jnp.concatenate(
        [(y * 2 + (core ^ step)) * vocab_rows + near for step in (0, 1) for y in (0, 1)]
    )

    own_count = jnp.sum(target_lengths).astype(jnp.float32)
    gain_part = jnp.concatenate(
        [norm_gains, jnp.full((1, norm_gains.shape[1]), own_count, jnp.float32)]
    )
    gain_part = lax.all_gather(gain_part, everywhere)
    count = jnp.sum(gain_part[::4, -1, 0])
    gains = gain_part[:, :-1].swapaxes(0, 1).reshape(norm_gains.shape[0], -1)

    hidden_rows = feed_out.shape[1]
    spare = ((0, 0), (0, -hidden_rows % 128))

    def attention_unit(layer):
        w_in = attention_in[layer].astype(half)
        w_in = w_in.reshape(w_in.shape[0], -1)
        return [w_in, attention_out[layer].T.astype(half)]

    def feed_units(layer):
        return [
            jnp.pad(feed_in[layer, :, 0].astype(half), spare),
            jnp.pad(feed_in[layer, :, 1].astype(half), spare),
            jnp.pad(feed_out[layer].T.astype(half), spare),
        ]

    def thirds(blocks, start):
        third = hidden_rows + spare[1][1]
        return [
            [b[:, start + k * third : start + (k + 1) * third] for b in blocks] for k in range(3)
        ]

    first = [u for layer in range(3) for u in attention_unit(layer)]
    first = gather_unit(jnp.concatenate(first + feed_units(0) + [table_pair], axis=1))
    second = gather_unit(jnp.concatenate(feed_units(1), axis=1))
    span = 4 * attention_out.shape[1]
    edge = first[0].shape[1] - 2 * vocab_rows
    attn = [[b[:, k * span : (k + 1) * span] for b in first] for k in range(3)]
    feed = (thirds(first, 3 * span), thirds(second, 0))
    near_pair = jnp.concatenate([b[:, edge:] for b in first], axis=1)
    table_pairs = [near_pair, flip(plain(near_pair), "c", 1)]
    table_pairs = [p[:, k * vocab_rows :][:, :vocab_rows] for p in table_pairs for k in range(4)]
    table_t = jnp.concatenate(table_pairs[::2], axis=1)
    w_head = jnp.concatenate(table_pairs[1::2], axis=1)

    source = lax.dynamic_index_in_dim(source_ids, row, 0, False)[0]
    target = lax.dynamic_index_in_dim(target_ids, row, 0, False)[0]
    source_len = lax.dynamic_index_in_dim(source_lengths, row, 0, False)[0]
    target_len = lax.dynamic_index_in_dim(target_lengths, row, 0, False)[0]
    src_rows = source.shape[0] // 2
    tgt_rows = target.shape[0] // 2
    src_pos = positions(src_rows)
    tgt_pos = positions(tgt_rows)
    key_bias = jnp.where(src_pos < source_len, 0.0, masked)[None, None, :]
    causal = jnp.where(tgt_pos[:, None] >= tgt_pos[None, :], 0.0, masked)[None]
    shifted = jnp.concatenate([jnp.zeros((1,), jnp.int32), target[:-1]])
    source_hot = (own_part(source, src_rows)[:, None] == vocab_ids[None, :]).astype(half)
    target_hot = (own_part(shifted, tgt_rows)[:, None] == vocab_ids[None, :]).astype(half)
    hits = own_part(target, tgt_rows)[:, None] == vocab_ids[None, :]

    src_embed = product_right(source_hot, table_t)
    src_norm_a = collect(normalize(src_embed, gains[0]))
    part, keep_src_a = self_attention(src_norm_a, attn[0], key_bias)
    src_mid = src_embed + fold(part)
    src_norm_b = collect(normalize(src_mid, gains[1]))
    part, keep_src_b = expand(src_norm_b, *feed[0])
    src_top = src_mid + fold(part)
    encoded = collect(normalize(src_top, gains[2]))

    tgt_embed = product_right(target_hot, table_t)
    tgt_norm_a = collect(normalize(tgt_embed, gains[3]))
    part, keep_tgt_a = self_attention(tgt_norm_a, attn[1], causal)
    tgt_self = tgt_embed + fold(part)
    tgt_norm_b = collect(normalize(tgt_self, gains[4]))
    part, keep_tgt_b = cross_attention(tgt_norm_b, encoded, attn[2], key_bias)
    tgt_cross = tgt_self + fold(part)
    tgt_norm_c = collect(normalize(tgt_cross, gains[5]))
    part, keep_tgt_c = expand(tgt_norm_c, *feed[1])
    tgt_top = tgt_cross + fold(part)
    tgt_norm_d = normalize(tgt_top, gains[6])

    logits = product(tgt_norm_d, w_head)
    peak = jnp.max(logits, axis=-1, keepdims=True)
    lse = peak + jnp.log(jnp.sum(jnp.exp(logits - peak), axis=-1, keepdims=True))
    picked = jnp.sum(jnp.where(hits, logits, 0.0), axis=-1, keepdims=True)
    weight = (tgt_pos[:tgt_rows] < target_len).astype(jnp.float32)[:, None] / count
    own_loss = jnp.sum((lse - picked) * weight)
    d_logits = ((jnp.exp(logits - lse) - hits.astype(jnp.float32)) * weight).astype(half)
    g_head = product_left(tgt_norm_d, d_logits).astype(half)

    d_tgt, gain_six = norm_back(tgt_top, gains[6], product_right(d_logits, w_head))
    *feed_one, d_in = expand_back(tgt_norm_c, *feed[1], keep_tgt_c, collect(d_tgt.astype(half)))
    feed_one = scatter_unit(feed_one)
    d_more, gain_five = norm_back(tgt_cross, gains[5], fold(d_in))
    d_tgt = d_tgt + d_more
    attn_two, d_query, d_keys = cross_attention_back(
        tgt_norm_b, encoded, attn[2], key_bias, keep_tgt_b, collect(d_tgt.astype(half))
    )
    attn_two = scatter_pairs(attn_two)
    d_encoded = fold(d_keys)
    d_more, gain_four = norm_back(tgt_self, gains[4], fold(d_query))
    d_tgt = d_tgt + d_more
    attn_one, d_in = self_attention_back(
        tgt_norm_a, attn[1], causal, keep_tgt_a, collect(d_tgt.astype(half))
    )
    attn_one = scatter_pairs(attn_one)
    d_more, gain_three = norm_back(tgt_embed, gains[3], fold(d_in))
    d_tgt = d_tgt + d_more

    d_src, gain_two = norm_back(src_top, gains[2], d_encoded)
    *feed_zero, d_in = expand_back(src_norm_b, *feed[0], keep_src_b, collect(d_src.astype(half)))
    feed_zero = scatter_unit(feed_zero)
    d_more, gain_one = norm_back(src_mid, gains[1], fold(d_in))
    d_src = d_src + d_more
    attn_zero, d_in = self_attention_back(
        src_norm_a, attn[0], key_bias, keep_src_a, collect(d_src.astype(half))
    )
    attn_zero = scatter_pairs(attn_zero)
    d_more, gain_zero = norm_back(src_embed, gains[0], fold(d_in))
    d_src = d_src + d_more

    g_table = product_left(d_src.astype(half), source_hot)
    g_table = (g_table + product_left(d_tgt.astype(half), target_hot)).astype(half)
    pairs = [g[:, k * vocab_rows :][:, :vocab_rows] for k in range(4) for g in (g_table, g_head)]
    pairs = [jnp.concatenate(pairs[k : k + 2], axis=1) for k in range(0, 8, 2)]
    pairs = jnp.concatenate([plain(p) for p in pairs], axis=0)
    rows = pairs.shape[0] // 2
    pairs = pairs[:rows].astype(jnp.float32) + flip(pairs[rows:], "c", 1).astype(jnp.float32)
    pairs = pairs.astype(half)
    pair_grad = scatter_pairs([pairs[: rows // 2], pairs[rows // 2 :]])

    g_gains = jnp.stack([gain_zero, gain_one, gain_two, gain_three, gain_four, gain_five, gain_six])
    g_gains = scatter_rows(g_gains.T, jnp.float32)
    g_gains = split_rows(split_rows(g_gains, "y", 1), "c", 1).T

    width = attention_out.shape[1]
    attn_grads = [attn_zero, attn_one, attn_two]
    units = [pair_grad, *attn_grads, feed_zero, feed_one]
    squares = sum(jnp.sum(g * g) for g in units) + jnp.sum(g_gains * g_gains)
    feed_grads = [thirds([g], 0) for g in (feed_zero, feed_one)]
    squares, loss = total_over(jnp.stack([squares, own_loss]), everywhere)
    attn_in = [g[:, : 3 * width].reshape(-1, 3, width) for g in attn_grads]
    gates_uppers = [
        jnp.stack([gate[0][:, :hidden_rows], upper[0][:, :hidden_rows]], axis=1)
        for gate, upper, _ in feed_grads
    ]
    downs = [down[0][:, :hidden_rows].T for _, _, down in feed_grads]
    grads = (
        plain(pair_grad[:, :vocab_rows].T),
        plain(pair_grad[:, vocab_rows:]),
        ordered(jnp.stack(attn_in), (0, 2, 1, 3)),
        plain(jnp.stack([g[:, 3 * width :].T for g in attn_grads])),
        plain(jnp.stack(gates_uppers)),
        ordered(jnp.stack(downs), (0, 2, 1)),
        g_gains,
    )
    grad_norm = jnp.sqrt(squares)
    scale = jnp.minimum(1.0, clip_limit / grad_norm)
    results = [
        adam(w, g * scale, m, v, r)
        for w, g, m, v, r in zip(masters, grads, firsts, seconds, step_rates)
    ]
    return (loss, grad_norm) + tuple(r[i] for i in range(3) for r in results)


def solution(mesh):
    shape = (mesh.shape["dp"] // 2, 2, mesh.shape["mp"] // 2, 2)
    inner = Mesh(np.asarray(mesh.devices).reshape(shape), ("far", "near", "y", "c"))
    dp = ("far", "near")
    mp = ("y", "c")
    params = (
        P(mp, dp),
        P(dp, mp),
        P(None, dp, None, mp),
        P(None, mp, dp),
        P(None, dp, None, mp),
        P(None, mp, dp),
        P(None, dp + mp),
    )
    ids = (P(None, dp, None), P(None, dp, None), P(None, dp), P(None, dp))
    return jax.shard_map(
        on_device,
        mesh=inner,
        in_specs=ids + params * 3,
        out_specs=(P(), P()) + params * 3,
        check_vma=False,
    )
```

```python
import jax
import jax.numpy as jnp
import numpy as np
from jax import lax
from jax.experimental.layout import Layout, with_layout_constraint
from jax.sharding import Mesh
from jax.sharding import PartitionSpec as P

DK = 64
STEP = 10


norm_eps = 1e-06
clip_limit = 0.05
step_rates = (0.4, 0.02, 0.02, 0.1, 0.02, 0.02, 0.25)
beta_one = 0.9
beta_two = 0.999
adam_eps = 1e-08
decay = 0.01
masked = -1000000000.0

half = jnp.bfloat16


def spin(part, axis, shift):
    size = lax.axis_size(axis)
    return lax.ppermute(part, axis, [(i, (i + shift) % size) for i in range(size)])


def flip(part, axis, bit):
    size = lax.axis_size(axis)
    return lax.ppermute(part, axis, [(i, i ^ bit) for i in range(size)])


def plain(part):
    return with_layout_constraint(part, Layout(major_to_minor=tuple(range(part.ndim))))


def ordered(part, order):
    return with_layout_constraint(part, Layout(major_to_minor=order))


def gather_unit(part):
    return lax.all_gather(plain(part), ("y", "near", "far"), axis=0, tiled=True)


def halves(whole):
    rows = whole.shape[0] // 2
    return [whole[:rows], whole[rows:]]


def place(part, other, axis, bit):
    first = (lax.axis_index(axis) // bit) % 2 == 0
    return [jnp.where(first, part, other), jnp.where(first, other, part)]


def join_rows(part, axis, bit):
    part = plain(part)
    return jnp.concatenate(place(part, flip(part, axis, bit), axis, bit), axis=0)


def gather_pairs(part, row_first):
    bit = 1
    while bit < lax.axis_size("far"):
        part = join_rows(part, "far", bit)
        bit *= 2
    if not row_first:
        part = plain(join_rows(part, "near", 1))
        return place(part, flip(part, "y", 1), "y", 1)
    part = plain(part)
    both = plain(jnp.concatenate([part, flip(part, "y", 1)], axis=0))
    pairs = zip(halves(both), halves(flip(both, "near", 1)))
    own, other = [jnp.concatenate(place(p, q, "near", 1), axis=0) for p, q in pairs]
    return place(own, other, "y", 1)


def scatter_unit(blocks, whole):
    rows, columns = blocks[0][0].shape
    for k, pair in enumerate(blocks):
        for y, part in enumerate(pair):
            whole = lax.dynamic_update_slice(whole, plain(part), (y * rows, k * columns))
    part = lax.psum_scatter(
        plain(whole), ("y", "near", "far"), scatter_dimension=0, tiled=True
    )
    return part.astype(jnp.float32)


def choose(parts, axis):
    first = lax.axis_index(axis) == 0
    own = jnp.where(first, parts[0], parts[1]).astype(jnp.float32)
    sent = plain(jnp.where(first, parts[1], parts[0]))
    return own + flip(sent, axis, 1).astype(jnp.float32)


def split_rows(whole, axis, bit):
    rows = whole.shape[0] // 2
    mine = (lax.axis_index(axis) // bit) % 2
    own = lax.dynamic_slice_in_dim(whole, mine * rows, rows)
    sent = plain(lax.dynamic_slice_in_dim(whole, (1 - mine) * rows, rows))
    return own.astype(jnp.float32) + flip(sent, axis, bit).astype(jnp.float32)


def scatter_rows(part, kind):
    part = split_rows(part.astype(kind), "near", 1)
    bit = lax.axis_size("far") // 2
    while bit:
        part = split_rows(part.astype(kind), "far", bit)
        bit //= 2
    return part


def scatter_pairs(parts):
    return scatter_rows(choose([plain(p) for p in parts], "y"), half)


def total_over(value, axes):
    for axis in axes:
        bit = 1
        while bit < lax.axis_size(axis):
            value = value + flip(value, axis, bit)
            bit *= 2
    return value


def collect(own):
    return jnp.concatenate([own, spin(own, "c", 1)], axis=0)


def fold(part):
    rows = part.shape[0] // 2
    return part[:rows] + spin(part[rows:].astype(half), "c", 1).astype(jnp.float32)


def product(left, right):
    return jnp.dot(left, right, preferred_element_type=jnp.float32)


def product_left(left, right):
    return lax.dot_general(
        left, right, (((0,), (0,)), ((), ())), preferred_element_type=jnp.float32
    )


def product_right(left, right):
    return lax.dot_general(
        left, right, (((1,), (1,)), ((), ())), preferred_element_type=jnp.float32
    )


def rms_norm(stream, gain):
    return stream * lax.rsqrt(jnp.mean(stream * stream, axis=-1, keepdims=True) + norm_eps) * gain


def normalize(stream, gain):
    return rms_norm(stream, gain).astype(half)


def norm_back(stream, gain, grad):
    _, pull = jax.vjp(rms_norm, stream, gain)
    return pull(grad)


def heads(flat):
    return flat.reshape(flat.shape[0], -1, DK)


def score_block(query, key, bias):
    return (
        jnp.einsum("rhd,shd->hrs", heads(query), heads(key), preferred_element_type=jnp.float32)
        * 0.125
        + bias
    )


def attend(query, key, value, bias):
    scores = score_block(query, key, bias)
    peak = jnp.max(scores, axis=-1, keepdims=True)
    raw = jnp.exp(scores - peak)
    total = jnp.sum(raw, axis=-1, keepdims=True)
    probs = (raw / total).astype(half)
    mixed = jnp.einsum("hrs,shd->rhd", probs, heads(value), preferred_element_type=jnp.float32)
    mixed = mixed.reshape(query.shape[0], -1).astype(half)
    return mixed, peak + jnp.log(total)


def attend_back(query, key, value, lse, bias, d_mixed):
    rows = query.shape[0]
    cols = key.shape[0]
    d_heads = heads(d_mixed)
    probs = jnp.exp(score_block(query, key, bias) - lse)
    d_value = jnp.einsum(
        "hrs,rhd->shd", probs.astype(half), d_heads, preferred_element_type=jnp.float32
    )
    d_probs = jnp.einsum("rhd,shd->hrs", d_heads, heads(value), preferred_element_type=jnp.float32)
    d_scores = (probs * (d_probs - jnp.sum(probs * d_probs, axis=-1, keepdims=True))).astype(half)
    d_query = (
        jnp.einsum("hrs,shd->rhd", d_scores, heads(key), preferred_element_type=jnp.float32) * 0.125
    )
    d_key = (
        jnp.einsum("hrs,rhd->shd", d_scores, heads(query), preferred_element_type=jnp.float32)
        * 0.125
    )
    return (
        d_query.reshape(rows, -1).astype(half),
        d_key.reshape(cols, -1).astype(half),
        d_value.reshape(cols, -1).astype(half),
    )


def self_attention(x_in, blocks, bias):
    part = 0.0
    kept = []
    for block in blocks:
        width = block.shape[1] // 4
        qkv = product(x_in, block[:, : 3 * width]).astype(half)
        query, key, value = qkv[:, :width], qkv[:, width : 2 * width], qkv[:, 2 * width :]
        mixed, lse = attend(query, key, value, bias)
        part = part + product_right(mixed, block[:, 3 * width :])
        kept.append((query, key, value, lse, mixed))
    return part, kept


def self_attention_back(x_in, blocks, bias, kept, d_full):
    d_in = 0.0
    grads = []
    for block, (query, key, value, lse, mixed) in zip(blocks, kept):
        width = block.shape[1] // 4
        g_out = product_left(d_full, mixed).astype(half)
        d_mixed = product(d_full, block[:, 3 * width :]).astype(half)
        d_qkv = jnp.concatenate(attend_back(query, key, value, lse, bias, d_mixed), axis=1)
        g_in = product_left(x_in, d_qkv).astype(half)
        grads.append(jnp.concatenate([g_in, g_out], axis=1))
        d_in = d_in + product_right(d_qkv, block[:, : 3 * width])
    return grads, d_in


def cross_attention(x_in, x_keys, blocks, bias):
    part = 0.0
    kept = []
    for block in blocks:
        width = block.shape[1] // 4
        query = product(x_in, block[:, :width]).astype(half)
        pair = product(x_keys, block[:, width : 3 * width]).astype(half)
        key, value = pair[:, :width], pair[:, width:]
        mixed, lse = attend(query, key, value, bias)
        part = part + product_right(mixed, block[:, 3 * width :])
        kept.append((query, key, value, lse, mixed))
    return part, kept


def cross_attention_back(x_in, x_keys, blocks, bias, kept, d_full):
    d_in = 0.0
    d_keys = 0.0
    grads = []
    for block, (query, key, value, lse, mixed) in zip(blocks, kept):
        width = block.shape[1] // 4
        g_out = product_left(d_full, mixed).astype(half)
        d_mixed = product(d_full, block[:, 3 * width :]).astype(half)
        d_query, d_key, d_value = attend_back(query, key, value, lse, bias, d_mixed)
        d_pair = jnp.concatenate([d_key, d_value], axis=1)
        g_query = product_left(x_in, d_query).astype(half)
        g_pair = product_left(x_keys, d_pair).astype(half)
        grads.append(jnp.concatenate([g_query, g_pair, g_out], axis=1))
        d_in = d_in + product_right(d_query, block[:, :width])
        d_keys = d_keys + product_right(d_pair, block[:, width : 3 * width])
    return grads, d_in, d_keys


def gated(gate, upper):
    return jax.nn.gelu(gate, approximate=True) * upper


def expand(x_in, gates, uppers, downs):
    part = 0.0
    kept = []
    for w_gate, w_upper, w_down in zip(gates, uppers, downs):
        gate = product(x_in, w_gate)
        upper = product(x_in, w_upper)
        hidden = gated(gate, upper).astype(half)
        part = part + product_right(hidden, w_down)
        kept.append((gate, upper, hidden))
    return part, kept


def expand_back(x_in, gates, uppers, downs, kept, d_full):
    d_in = 0.0
    g_gates, g_uppers, g_downs = [], [], []
    for w_gate, w_upper, w_down, (gate, upper, hidden) in zip(gates, uppers, downs, kept):
        g_downs.append(product_left(d_full, hidden).astype(half))
        _, pull = jax.vjp(gated, gate, upper)
        d_gate, d_upper = pull(product(d_full, w_down))
        d_gate = d_gate.astype(half)
        d_upper = d_upper.astype(half)
        g_gates.append(product_left(x_in, d_gate).astype(half))
        g_uppers.append(product_left(x_in, d_upper).astype(half))
        d_in = d_in + product_right(d_gate, w_gate) + product_right(d_upper, w_upper)
    return g_gates, g_uppers, g_downs, d_in


def adam(weight, grad, first, second, step_rate):
    first = beta_one * first + (1 - beta_one) * grad
    second = beta_two * second + (1 - beta_two) * grad * grad
    step_size = first / (1 - beta_one**STEP) / (jnp.sqrt(second / (1 - beta_two**STEP)) + adam_eps)
    return (weight - step_rate * (step_size + decay * weight), first, second)


def own_part(whole, rows):
    return lax.dynamic_slice_in_dim(whole, lax.axis_index("c") * rows, rows)


def positions(rows):
    core = lax.axis_index("c")
    near = jnp.arange(rows, dtype=jnp.int32)
    return jnp.concatenate([core * rows + near, (1 - core) * rows + near])


def on_device(*args):
    source_ids, target_ids, source_lengths, target_lengths = args[:4]
    masters, firsts, seconds = args[4:11], args[11:18], args[18:25]
    embedding, unembedding, attention_in, attention_out, feed_in, feed_out, norm_gains = masters
    row = lax.axis_index("y")
    core = lax.axis_index("c")
    everywhere = ("near", "far", "y", "c")

    vocab_rows = embedding.shape[0]
    table_pair = jnp.concatenate([embedding.T.astype(half), unembedding.astype(half)], axis=1)
    near = jnp.arange(vocab_rows, dtype=jnp.int32)
    vocab_ids = jnp.concatenate(
        [(y * 2 + (core ^ step)) * vocab_rows + near for step in (0, 1) for y in (0, 1)]
    )

    own_count = jnp.sum(target_lengths).astype(jnp.float32)
    gain_part = jnp.concatenate(
        [norm_gains, jnp.full((1, norm_gains.shape[1]), own_count, jnp.float32)]
    )
    gain_part = lax.all_gather(gain_part, everywhere)
    count = jnp.sum(gain_part[::4, -1, 0])
    gains = gain_part[:, :-1].swapaxes(0, 1).reshape(norm_gains.shape[0], -1)

    hidden_rows = feed_out.shape[1]
    spare = ((0, 0), (0, -hidden_rows % 128))

    def attention_unit(layer):
        w_in = attention_in[layer].astype(half)
        w_in = w_in.reshape(w_in.shape[0], -1)
        return [w_in, attention_out[layer].T.astype(half)]

    def feed_units(layer):
        return [
            jnp.pad(feed_in[layer, :, 0].astype(half), spare),
            jnp.pad(feed_in[layer, :, 1].astype(half), spare),
            jnp.pad(feed_out[layer].T.astype(half), spare),
        ]

    def thirds(blocks, start):
        third = hidden_rows + spare[1][1]
        return [
            [b[:, start + k * third : start + (k + 1) * third] for b in blocks] for k in range(3)
        ]

    first = gather_unit(jnp.concatenate(feed_units(0) + [table_pair], axis=1))
    second = halves(gather_unit(jnp.concatenate(feed_units(1), axis=1)))
    attn = [
        gather_pairs(jnp.concatenate(attention_unit(layer), axis=1), row_first)
        for layer, row_first in enumerate((False, True, False))
    ]
    fills = (jnp.minimum(jnp.sum(target_lengths), 0), jnp.minimum(jnp.sum(source_lengths), 0))
    blanks = [jnp.full((2 * b.shape[0], b.shape[1]), f.astype(half)) for b, f in zip(second, fills)]
    first, attn, blanks = lax.optimization_barrier((first, attn, blanks))
    first = halves(first)
    edge = first[0].shape[1] - 2 * vocab_rows
    feed = (thirds(first, 0), thirds(second, 0))
    near_pair = jnp.concatenate([b[:, edge:] for b in first], axis=1)
    table_pairs = [near_pair, flip(plain(near_pair), "c", 1)]
    table_pairs = [p[:, k * vocab_rows :][:, :vocab_rows] for p in table_pairs for k in range(4)]
    table_t = jnp.concatenate(table_pairs[::2], axis=1)
    w_head = jnp.concatenate(table_pairs[1::2], axis=1)

    source = lax.dynamic_index_in_dim(source_ids, row, 0, False)[0]
    target = lax.dynamic_index_in_dim(target_ids, row, 0, False)[0]
    source_len = lax.dynamic_index_in_dim(source_lengths, row, 0, False)[0]
    target_len = lax.dynamic_index_in_dim(target_lengths, row, 0, False)[0]
    src_rows = source.shape[0] // 2
    tgt_rows = target.shape[0] // 2
    src_pos = positions(src_rows)
    tgt_pos = positions(tgt_rows)
    key_bias = jnp.where(src_pos < source_len, 0.0, masked)[None, None, :]
    causal = jnp.where(tgt_pos[:, None] >= tgt_pos[None, :], 0.0, masked)[None]
    shifted = jnp.concatenate([jnp.zeros((1,), jnp.int32), target[:-1]])
    source_hot = (own_part(source, src_rows)[:, None] == vocab_ids[None, :]).astype(half)
    target_hot = (own_part(shifted, tgt_rows)[:, None] == vocab_ids[None, :]).astype(half)
    hits = own_part(target, tgt_rows)[:, None] == vocab_ids[None, :]

    src_embed = product_right(source_hot, table_t)
    src_norm_a = collect(normalize(src_embed, gains[0]))
    part, keep_src_a = self_attention(src_norm_a, attn[0], key_bias)
    src_mid = src_embed + fold(part)
    src_norm_b = collect(normalize(src_mid, gains[1]))
    part, keep_src_b = expand(src_norm_b, *feed[0])
    src_top = src_mid + fold(part)
    encoded = collect(normalize(src_top, gains[2]))

    tgt_embed = product_right(target_hot, table_t)
    tgt_norm_a = collect(normalize(tgt_embed, gains[3]))
    part, keep_tgt_a = self_attention(tgt_norm_a, attn[1], causal)
    tgt_self = tgt_embed + fold(part)
    tgt_norm_b = collect(normalize(tgt_self, gains[4]))
    part, keep_tgt_b = cross_attention(tgt_norm_b, encoded, attn[2], key_bias)
    tgt_cross = tgt_self + fold(part)
    tgt_norm_c = collect(normalize(tgt_cross, gains[5]))
    part, keep_tgt_c = expand(tgt_norm_c, *feed[1])
    tgt_top = tgt_cross + fold(part)
    tgt_norm_d = normalize(tgt_top, gains[6])

    logits = product(tgt_norm_d, w_head)
    peak = jnp.max(logits, axis=-1, keepdims=True)
    lse = peak + jnp.log(jnp.sum(jnp.exp(logits - peak), axis=-1, keepdims=True))
    picked = jnp.sum(jnp.where(hits, logits, 0.0), axis=-1, keepdims=True)
    weight = (tgt_pos[:tgt_rows] < target_len).astype(jnp.float32)[:, None] / count
    own_loss = jnp.sum((lse - picked) * weight)
    d_logits = ((jnp.exp(logits - lse) - hits.astype(jnp.float32)) * weight).astype(half)
    g_head = product_left(tgt_norm_d, d_logits).astype(half)

    d_tgt, gain_six = norm_back(tgt_top, gains[6], product_right(d_logits, w_head))
    *feed_one, d_in = expand_back(tgt_norm_c, *feed[1], keep_tgt_c, collect(d_tgt.astype(half)))
    feed_one = scatter_unit(feed_one, blanks[1])
    d_more, gain_five = norm_back(tgt_cross, gains[5], fold(d_in))
    d_tgt = d_tgt + d_more
    attn_two, d_query, d_keys = cross_attention_back(
        tgt_norm_b, encoded, attn[2], key_bias, keep_tgt_b, collect(d_tgt.astype(half))
    )
    attn_two = scatter_pairs(attn_two)
    d_encoded = fold(d_keys)
    d_more, gain_four = norm_back(tgt_self, gains[4], fold(d_query))
    d_tgt = d_tgt + d_more
    attn_one, d_in = self_attention_back(
        tgt_norm_a, attn[1], causal, keep_tgt_a, collect(d_tgt.astype(half))
    )
    attn_one = scatter_pairs(attn_one)
    d_more, gain_three = norm_back(tgt_embed, gains[3], fold(d_in))
    d_tgt = d_tgt + d_more

    d_src, gain_two = norm_back(src_top, gains[2], d_encoded)
    *feed_zero, d_in = expand_back(src_norm_b, *feed[0], keep_src_b, collect(d_src.astype(half)))
    feed_zero = scatter_unit(feed_zero, blanks[0])
    d_more, gain_one = norm_back(src_mid, gains[1], fold(d_in))
    d_src = d_src + d_more
    attn_zero, d_in = self_attention_back(
        src_norm_a, attn[0], key_bias, keep_src_a, collect(d_src.astype(half))
    )
    attn_zero = scatter_pairs(attn_zero)
    d_more, gain_zero = norm_back(src_embed, gains[0], fold(d_in))
    d_src = d_src + d_more

    g_table = product_left(d_src.astype(half), source_hot)
    g_table = (g_table + product_left(d_tgt.astype(half), target_hot)).astype(half)
    pairs = [g[:, k * vocab_rows :][:, :vocab_rows] for k in range(4) for g in (g_table, g_head)]
    pairs = [jnp.concatenate(pairs[k : k + 2], axis=1) for k in range(0, 8, 2)]
    pairs = jnp.concatenate([plain(p) for p in pairs], axis=0)
    rows = pairs.shape[0] // 2
    pairs = pairs[:rows].astype(jnp.float32) + flip(pairs[rows:], "c", 1).astype(jnp.float32)
    pairs = pairs.astype(half)
    pair_grad = scatter_pairs([pairs[: rows // 2], pairs[rows // 2 :]])

    g_gains = jnp.stack([gain_zero, gain_one, gain_two, gain_three, gain_four, gain_five, gain_six])
    g_gains = scatter_rows(g_gains.T, jnp.float32)
    g_gains = split_rows(split_rows(g_gains, "y", 1), "c", 1).T

    width = attention_out.shape[1]
    attn_grads = [attn_zero, attn_one, attn_two]
    units = [pair_grad, *attn_grads, feed_zero, feed_one]
    squares = sum(jnp.sum(g * g) for g in units) + jnp.sum(g_gains * g_gains)
    feed_grads = [thirds([g], 0) for g in (feed_zero, feed_one)]
    squares, loss = total_over(jnp.stack([squares, own_loss]), everywhere)
    attn_in = [g[:, : 3 * width].reshape(-1, 3, width) for g in attn_grads]
    gates_uppers = [
        jnp.stack([gate[0][:, :hidden_rows], upper[0][:, :hidden_rows]], axis=1)
        for gate, upper, _ in feed_grads
    ]
    downs = [down[0][:, :hidden_rows].T for _, _, down in feed_grads]
    grads = (
        plain(pair_grad[:, :vocab_rows].T),
        plain(pair_grad[:, vocab_rows:]),
        ordered(jnp.stack(attn_in), (0, 2, 1, 3)),
        plain(jnp.stack([g[:, 3 * width :].T for g in attn_grads])),
        plain(jnp.stack(gates_uppers)),
        ordered(jnp.stack(downs), (0, 2, 1)),
        g_gains,
    )
    grad_norm = jnp.sqrt(squares)
    scale = jnp.minimum(1.0, clip_limit / grad_norm)
    results = [
        adam(w, g * scale, m, v, r)
        for w, g, m, v, r in zip(masters, grads, firsts, seconds, step_rates)
    ]
    return (loss, grad_norm) + tuple(r[i] for i in range(3) for r in results)


def solution(mesh):
    shape = (mesh.shape["dp"] // 2, 2, mesh.shape["mp"] // 2, 2)
    inner = Mesh(np.asarray(mesh.devices).reshape(shape), ("far", "near", "y", "c"))
    dp = ("far", "near")
    mp = ("y", "c")
    params = (
        P(mp, dp),
        P(dp, mp),
        P(None, dp, None, mp),
        P(None, mp, dp),
        P(None, dp, None, mp),
        P(None, mp, dp),
        P(None, dp + mp),
    )
    ids = (P(None, dp, None), P(None, dp, None), P(None, dp), P(None, dp))
    return jax.shard_map(
        on_device,
        mesh=inner,
        in_specs=ids + params * 3,
        out_specs=(P(), P()) + params * 3,
        check_vma=False,
    )
```

```python
import jax
import jax.numpy as jnp
import numpy as np
from jax import lax
from jax.experimental.layout import Layout, with_layout_constraint
from jax.sharding import Mesh
from jax.sharding import PartitionSpec as P

DK = 64
STEP = 10


norm_eps = 1e-06
clip_limit = 0.05
step_rates = (0.4, 0.02, 0.02, 0.1, 0.02, 0.02, 0.25)
beta_one = 0.9
beta_two = 0.999
adam_eps = 1e-08
decay = 0.01
masked = -1000000000.0

half = jnp.bfloat16


def spin(part, axis, shift):
    size = lax.axis_size(axis)
    return lax.ppermute(part, axis, [(i, (i + shift) % size) for i in range(size)])


def flip(part, axis, bit):
    size = lax.axis_size(axis)
    return lax.ppermute(part, axis, [(i, i ^ bit) for i in range(size)])


def plain(part):
    return with_layout_constraint(part, Layout(major_to_minor=tuple(range(part.ndim))))


def ordered(part, order):
    return with_layout_constraint(part, Layout(major_to_minor=order))


def gather_unit(part):
    return lax.all_gather(plain(part), ("y", "near", "far"), axis=0, tiled=True)


def halves(whole):
    rows = whole.shape[0] // 2
    return [whole[:rows], whole[rows:]]


def place(part, other, axis, bit):
    first = (lax.axis_index(axis) // bit) % 2 == 0
    return [jnp.where(first, part, other), jnp.where(first, other, part)]


def join_rows(part, axis, bit):
    part = plain(part)
    return jnp.concatenate(place(part, flip(part, axis, bit), axis, bit), axis=0)


def gather_pairs(part, row_first):
    bit = 1
    while bit < lax.axis_size("far"):
        part = join_rows(part, "far", bit)
        bit *= 2
    if not row_first:
        part = plain(join_rows(part, "near", 1))
        return place(part, flip(part, "y", 1), "y", 1)
    part = plain(part)
    both = plain(jnp.concatenate([part, flip(part, "y", 1)], axis=0))
    pairs = zip(halves(both), halves(flip(both, "near", 1)))
    own, other = [jnp.concatenate(place(p, q, "near", 1), axis=0) for p, q in pairs]
    return place(own, other, "y", 1)


def scatter_unit(blocks, whole):
    rows, columns = blocks[0][0].shape
    for k, pair in enumerate(blocks):
        for y, part in enumerate(pair):
            whole = lax.dynamic_update_slice(whole, plain(part), (y * rows, k * columns))
    part = lax.psum_scatter(
        plain(whole), ("y", "near", "far"), scatter_dimension=0, tiled=True
    )
    return part.astype(jnp.float32)


def choose(parts, axis):
    first = lax.axis_index(axis) == 0
    own = jnp.where(first, parts[0], parts[1]).astype(jnp.float32)
    sent = plain(jnp.where(first, parts[1], parts[0]))
    return own + flip(sent, axis, 1).astype(jnp.float32)


def split_rows(whole, axis, bit):
    rows = whole.shape[0] // 2
    mine = (lax.axis_index(axis) // bit) % 2
    own = lax.dynamic_slice_in_dim(whole, mine * rows, rows)
    sent = plain(lax.dynamic_slice_in_dim(whole, (1 - mine) * rows, rows))
    return own.astype(jnp.float32) + flip(sent, axis, bit).astype(jnp.float32)


def scatter_rows(part, kind):
    part = split_rows(part.astype(kind), "near", 1)
    bit = lax.axis_size("far") // 2
    while bit:
        part = split_rows(part.astype(kind), "far", bit)
        bit //= 2
    return part


def scatter_pairs(parts):
    return scatter_rows(choose([plain(p) for p in parts], "y"), half)


def total_over(value, axes):
    for axis in axes:
        bit = 1
        while bit < lax.axis_size(axis):
            value = value + flip(value, axis, bit)
            bit *= 2
    return value


def collect(own):
    return jnp.concatenate([own, spin(own, "c", 1)], axis=0)


def fold(part):
    rows = part.shape[0] // 2
    return part[:rows] + spin(part[rows:].astype(half), "c", 1).astype(jnp.float32)


def product(left, right):
    return jnp.dot(left, right, preferred_element_type=jnp.float32)


def product_left(left, right):
    return lax.dot_general(
        left, right, (((0,), (0,)), ((), ())), preferred_element_type=jnp.float32
    )


def product_right(left, right):
    return lax.dot_general(
        left, right, (((1,), (1,)), ((), ())), preferred_element_type=jnp.float32
    )


def rms_norm(stream, gain):
    return stream * lax.rsqrt(jnp.mean(stream * stream, axis=-1, keepdims=True) + norm_eps) * gain


def normalize(stream, gain):
    return rms_norm(stream, gain).astype(half)


def norm_back(stream, gain, grad):
    _, pull = jax.vjp(rms_norm, stream, gain)
    return pull(grad)


def heads(flat):
    return flat.reshape(flat.shape[0], -1, DK)


def score_block(query, key, bias):
    return (
        jnp.einsum("rhd,shd->hrs", heads(query), heads(key), preferred_element_type=jnp.float32)
        * 0.125
        + bias
    )


def attend(query, key, value, bias):
    scores = score_block(query, key, bias)
    peak = jnp.max(scores, axis=-1, keepdims=True)
    raw = jnp.exp(scores - peak)
    total = jnp.sum(raw, axis=-1, keepdims=True)
    probs = (raw / total).astype(half)
    mixed = jnp.einsum("hrs,shd->rhd", probs, heads(value), preferred_element_type=jnp.float32)
    mixed = mixed.reshape(query.shape[0], -1).astype(half)
    return mixed, peak + jnp.log(total)


def attend_back(query, key, value, lse, bias, d_mixed):
    rows = query.shape[0]
    cols = key.shape[0]
    d_heads = heads(d_mixed)
    probs = jnp.exp(score_block(query, key, bias) - lse)
    d_value = jnp.einsum(
        "hrs,rhd->shd", probs.astype(half), d_heads, preferred_element_type=jnp.float32
    )
    d_probs = jnp.einsum("rhd,shd->hrs", d_heads, heads(value), preferred_element_type=jnp.float32)
    d_scores = (probs * (d_probs - jnp.sum(probs * d_probs, axis=-1, keepdims=True))).astype(half)
    d_query = (
        jnp.einsum("hrs,shd->rhd", d_scores, heads(key), preferred_element_type=jnp.float32) * 0.125
    )
    d_key = (
        jnp.einsum("hrs,rhd->shd", d_scores, heads(query), preferred_element_type=jnp.float32)
        * 0.125
    )
    return (
        d_query.reshape(rows, -1).astype(half),
        d_key.reshape(cols, -1).astype(half),
        d_value.reshape(cols, -1).astype(half),
    )


def self_attention(x_in, blocks, bias):
    part = 0.0
    kept = []
    for block in blocks:
        width = block.shape[1] // 4
        qkv = product(x_in, block[:, : 3 * width]).astype(half)
        query, key, value = qkv[:, :width], qkv[:, width : 2 * width], qkv[:, 2 * width :]
        mixed, lse = attend(query, key, value, bias)
        part = part + product_right(mixed, block[:, 3 * width :])
        kept.append((query, key, value, lse, mixed))
    return part, kept


def self_attention_back(x_in, blocks, bias, kept, d_full):
    d_in = 0.0
    grads = []
    for block, (query, key, value, lse, mixed) in zip(blocks, kept):
        width = block.shape[1] // 4
        g_out = product_left(d_full, mixed).astype(half)
        d_mixed = product(d_full, block[:, 3 * width :]).astype(half)
        d_qkv = jnp.concatenate(attend_back(query, key, value, lse, bias, d_mixed), axis=1)
        g_in = product_left(x_in, d_qkv).astype(half)
        grads.append(jnp.concatenate([g_in, g_out], axis=1))
        d_in = d_in + product_right(d_qkv, block[:, : 3 * width])
    return grads, d_in


def cross_attention(x_in, x_keys, blocks, bias):
    part = 0.0
    kept = []
    for block in blocks:
        width = block.shape[1] // 4
        query = product(x_in, block[:, :width]).astype(half)
        pair = product(x_keys, block[:, width : 3 * width]).astype(half)
        key, value = pair[:, :width], pair[:, width:]
        mixed, lse = attend(query, key, value, bias)
        part = part + product_right(mixed, block[:, 3 * width :])
        kept.append((query, key, value, lse, mixed))
    return part, kept


def cross_attention_back(x_in, x_keys, blocks, bias, kept, d_full):
    d_in = 0.0
    d_keys = 0.0
    grads = []
    for block, (query, key, value, lse, mixed) in zip(blocks, kept):
        width = block.shape[1] // 4
        g_out = product_left(d_full, mixed).astype(half)
        d_mixed = product(d_full, block[:, 3 * width :]).astype(half)
        d_query, d_key, d_value = attend_back(query, key, value, lse, bias, d_mixed)
        d_pair = jnp.concatenate([d_key, d_value], axis=1)
        g_query = product_left(x_in, d_query).astype(half)
        g_pair = product_left(x_keys, d_pair).astype(half)
        grads.append(jnp.concatenate([g_query, g_pair, g_out], axis=1))
        d_in = d_in + product_right(d_query, block[:, :width])
        d_keys = d_keys + product_right(d_pair, block[:, width : 3 * width])
    return grads, d_in, d_keys


def gated(gate, upper):
    return jax.nn.gelu(gate, approximate=True) * upper


def expand(x_in, gates, uppers, downs):
    part = 0.0
    kept = []
    for w_gate, w_upper, w_down in zip(gates, uppers, downs):
        gate = product(x_in, w_gate)
        upper = product(x_in, w_upper)
        hidden = gated(gate, upper).astype(half)
        part = part + product_right(hidden, w_down)
        kept.append((gate, upper, hidden))
    return part, kept


def expand_back(x_in, gates, uppers, downs, kept, d_full):
    d_in = 0.0
    g_gates, g_uppers, g_downs = [], [], []
    for w_gate, w_upper, w_down, (gate, upper, hidden) in zip(gates, uppers, downs, kept):
        g_downs.append(product_left(d_full, hidden).astype(half))
        _, pull = jax.vjp(gated, gate, upper)
        d_gate, d_upper = pull(product(d_full, w_down))
        d_gate = d_gate.astype(half)
        d_upper = d_upper.astype(half)
        g_gates.append(product_left(x_in, d_gate).astype(half))
        g_uppers.append(product_left(x_in, d_upper).astype(half))
        d_in = d_in + product_right(d_gate, w_gate) + product_right(d_upper, w_upper)
    return g_gates, g_uppers, g_downs, d_in


def adam(weight, grad, first, second, step_rate):
    first = beta_one * first + (1 - beta_one) * grad
    second = beta_two * second + (1 - beta_two) * grad * grad
    step_size = first / (1 - beta_one**STEP) / (jnp.sqrt(second / (1 - beta_two**STEP)) + adam_eps)
    return (weight - step_rate * (step_size + decay * weight), first, second)


def own_part(whole, rows):
    return lax.dynamic_slice_in_dim(whole, lax.axis_index("c") * rows, rows)


def positions(rows):
    core = lax.axis_index("c")
    near = jnp.arange(rows, dtype=jnp.int32)
    return jnp.concatenate([core * rows + near, (1 - core) * rows + near])


def on_device(*args):
    source_ids, target_ids, source_lengths, target_lengths = args[:4]
    masters, firsts, seconds = args[4:11], args[11:18], args[18:25]
    embedding, unembedding, attention_in, attention_out, feed_in, feed_out, norm_gains = masters
    row = lax.axis_index("y")
    core = lax.axis_index("c")
    everywhere = ("near", "far", "y", "c")

    vocab_rows = embedding.shape[0]
    table_pair = jnp.concatenate([embedding.T.astype(half), unembedding.astype(half)], axis=1)
    near = jnp.arange(vocab_rows, dtype=jnp.int32)
    vocab_ids = jnp.concatenate(
        [(y * 2 + (core ^ step)) * vocab_rows + near for step in (0, 1) for y in (0, 1)]
    )

    own_count = jnp.sum(target_lengths).astype(jnp.float32)
    gain_part = jnp.concatenate(
        [norm_gains, jnp.full((1, norm_gains.shape[1]), own_count, jnp.float32)]
    )
    gain_part = lax.all_gather(gain_part, everywhere)
    count = jnp.sum(gain_part[::4, -1, 0])
    gains = gain_part[:, :-1].swapaxes(0, 1).reshape(norm_gains.shape[0], -1)

    hidden_rows = feed_out.shape[1]
    spare = ((0, 0), (0, -hidden_rows % 128))

    def attention_unit(layer):
        w_in = attention_in[layer].astype(half)
        w_in = w_in.reshape(w_in.shape[0], -1)
        return [w_in, attention_out[layer].T.astype(half)]

    def feed_units(layer):
        return [
            jnp.pad(feed_in[layer, :, 0].astype(half), spare),
            jnp.pad(feed_in[layer, :, 1].astype(half), spare),
            jnp.pad(feed_out[layer].T.astype(half), spare),
        ]

    third = hidden_rows + spare[1][1]

    def thirds(blocks, start):
        return [
            [b[:, start + k * third : start + (k + 1) * third] for b in blocks] for k in range(3)
        ]

    first = plain(jnp.concatenate(feed_units(0) + [table_pair], axis=1))
    attn = [plain(jnp.concatenate(attention_unit(layer), axis=1)) for layer in range(3)]
    attn, gains = lax.optimization_barrier((attn, gains))
    first = gather_unit(first)
    second = halves(gather_unit(jnp.concatenate(feed_units(1), axis=1)))
    attn = [gather_pairs(a, row_first) for a, row_first in zip(attn, (False, True, False))]
    fills = (jnp.minimum(jnp.sum(target_lengths), 0), jnp.minimum(jnp.sum(source_lengths), 0))
    blanks = [jnp.full((first.shape[0], 2 * third), f.astype(half)) for f in fills]
    first, attn, blanks = lax.optimization_barrier((first, attn, blanks))
    first = halves(first)
    edge = first[0].shape[1] - 2 * vocab_rows
    feed = (thirds(first, 0), thirds(second, 0))
    near_pair = jnp.concatenate([b[:, edge:] for b in first], axis=1)
    table_pairs = [near_pair, flip(plain(near_pair), "c", 1)]
    table_pairs = [p[:, k * vocab_rows :][:, :vocab_rows] for p in table_pairs for k in range(4)]
    table_t = jnp.concatenate(table_pairs[::2], axis=1)
    w_head = jnp.concatenate(table_pairs[1::2], axis=1)

    source = lax.dynamic_index_in_dim(source_ids, row, 0, False)[0]
    target = lax.dynamic_index_in_dim(target_ids, row, 0, False)[0]
    source_len = lax.dynamic_index_in_dim(source_lengths, row, 0, False)[0]
    target_len = lax.dynamic_index_in_dim(target_lengths, row, 0, False)[0]
    src_rows = source.shape[0] // 2
    tgt_rows = target.shape[0] // 2
    src_pos = positions(src_rows)
    tgt_pos = positions(tgt_rows)
    key_bias = jnp.where(src_pos < source_len, 0.0, masked)[None, None, :]
    causal = jnp.where(tgt_pos[:, None] >= tgt_pos[None, :], 0.0, masked)[None]
    shifted = jnp.concatenate([jnp.zeros((1,), jnp.int32), target[:-1]])
    source_hot = (own_part(source, src_rows)[:, None] == vocab_ids[None, :]).astype(half)
    target_hot = (own_part(shifted, tgt_rows)[:, None] == vocab_ids[None, :]).astype(half)
    hits = own_part(target, tgt_rows)[:, None] == vocab_ids[None, :]

    src_embed = product_right(source_hot, table_t)
    src_norm_a = collect(normalize(src_embed, gains[0]))
    part, keep_src_a = self_attention(src_norm_a, attn[0], key_bias)
    src_mid = src_embed + fold(part)
    src_norm_b = collect(normalize(src_mid, gains[1]))
    part, keep_src_b = expand(src_norm_b, *feed[0])
    src_top = src_mid + fold(part)
    encoded = collect(normalize(src_top, gains[2]))

    tgt_embed = product_right(target_hot, table_t)
    tgt_norm_a = collect(normalize(tgt_embed, gains[3]))
    part, keep_tgt_a = self_attention(tgt_norm_a, attn[1], causal)
    tgt_self = tgt_embed + fold(part)
    tgt_norm_b = collect(normalize(tgt_self, gains[4]))
    part, keep_tgt_b = cross_attention(tgt_norm_b, encoded, attn[2], key_bias)
    tgt_cross = tgt_self + fold(part)
    tgt_norm_c = collect(normalize(tgt_cross, gains[5]))
    part, keep_tgt_c = expand(tgt_norm_c, *feed[1])
    tgt_top = tgt_cross + fold(part)
    tgt_norm_d = normalize(tgt_top, gains[6])

    logits = product(tgt_norm_d, w_head)
    peak = jnp.max(logits, axis=-1, keepdims=True)
    lse = peak + jnp.log(jnp.sum(jnp.exp(logits - peak), axis=-1, keepdims=True))
    picked = jnp.sum(jnp.where(hits, logits, 0.0), axis=-1, keepdims=True)
    weight = (tgt_pos[:tgt_rows] < target_len).astype(jnp.float32)[:, None] / count
    own_loss = jnp.sum((lse - picked) * weight)
    d_logits = ((jnp.exp(logits - lse) - hits.astype(jnp.float32)) * weight).astype(half)
    g_head = product_left(tgt_norm_d, d_logits).astype(half)

    d_tgt, gain_six = norm_back(tgt_top, gains[6], product_right(d_logits, w_head))
    *feed_one, d_in = expand_back(tgt_norm_c, *feed[1], keep_tgt_c, collect(d_tgt.astype(half)))
    down_one = scatter_pairs(feed_one[2])
    feed_one = scatter_unit(feed_one[:2], blanks[1])
    d_more, gain_five = norm_back(tgt_cross, gains[5], fold(d_in))
    d_tgt = d_tgt + d_more
    attn_two, d_query, d_keys = cross_attention_back(
        tgt_norm_b, encoded, attn[2], key_bias, keep_tgt_b, collect(d_tgt.astype(half))
    )
    attn_two = scatter_pairs(attn_two)
    d_encoded = fold(d_keys)
    d_more, gain_four = norm_back(tgt_self, gains[4], fold(d_query))
    d_tgt = d_tgt + d_more
    attn_one, d_in = self_attention_back(
        tgt_norm_a, attn[1], causal, keep_tgt_a, collect(d_tgt.astype(half))
    )
    attn_one = scatter_pairs(attn_one)
    d_more, gain_three = norm_back(tgt_embed, gains[3], fold(d_in))
    d_tgt = d_tgt + d_more

    d_src, gain_two = norm_back(src_top, gains[2], d_encoded)
    *feed_zero, d_in = expand_back(src_norm_b, *feed[0], keep_src_b, collect(d_src.astype(half)))
    down_zero = scatter_pairs(feed_zero[2])
    feed_zero = scatter_unit(feed_zero[:2], blanks[0])
    d_more, gain_one = norm_back(src_mid, gains[1], fold(d_in))
    d_src = d_src + d_more
    attn_zero, d_in = self_attention_back(
        src_norm_a, attn[0], key_bias, keep_src_a, collect(d_src.astype(half))
    )
    attn_zero = scatter_pairs(attn_zero)
    d_more, gain_zero = norm_back(src_embed, gains[0], fold(d_in))
    d_src = d_src + d_more

    g_table = product_left(d_src.astype(half), source_hot)
    g_table = (g_table + product_left(d_tgt.astype(half), target_hot)).astype(half)
    pairs = [g[:, k * vocab_rows :][:, :vocab_rows] for k in range(4) for g in (g_table, g_head)]
    pairs = [jnp.concatenate(pairs[k : k + 2], axis=1) for k in range(0, 8, 2)]
    pairs = jnp.concatenate([plain(p) for p in pairs], axis=0)
    rows = pairs.shape[0] // 2
    pairs = pairs[:rows].astype(jnp.float32) + flip(pairs[rows:], "c", 1).astype(jnp.float32)
    pairs = pairs.astype(half)
    pair_grad = scatter_pairs([pairs[: rows // 2], pairs[rows // 2 :]])

    g_gains = jnp.stack([gain_zero, gain_one, gain_two, gain_three, gain_four, gain_five, gain_six])
    g_gains = scatter_rows(g_gains.T, jnp.float32)
    g_gains = split_rows(split_rows(g_gains, "y", 1), "c", 1).T

    width = attention_out.shape[1]
    attn_grads = [attn_zero, attn_one, attn_two]
    units = [pair_grad, *attn_grads, feed_zero, feed_one, down_zero, down_one]
    squares = sum(jnp.sum(g * g) for g in units) + jnp.sum(g_gains * g_gains)
    squares, loss = total_over(jnp.stack([squares, own_loss]), everywhere)
    attn_in = [g[:, : 3 * width].reshape(-1, 3, width) for g in attn_grads]
    gates_uppers = [
        g.reshape(-1, 2, third)[..., :hidden_rows] for g in (feed_zero, feed_one)
    ]
    downs = [g[:, :hidden_rows].T for g in (down_zero, down_one)]
    grads = (
        plain(pair_grad[:, :vocab_rows].T),
        plain(pair_grad[:, vocab_rows:]),
        ordered(jnp.stack(attn_in), (0, 2, 1, 3)),
        plain(jnp.stack([g[:, 3 * width :].T for g in attn_grads])),
        plain(jnp.stack(gates_uppers)),
        ordered(jnp.stack(downs), (0, 2, 1)),
        g_gains,
    )
    grad_norm = jnp.sqrt(squares)
    scale = jnp.minimum(1.0, clip_limit / grad_norm)
    results = [
        adam(w, g * scale, m, v, r)
        for w, g, m, v, r in zip(masters, grads, firsts, seconds, step_rates)
    ]
    return (loss, grad_norm) + tuple(r[i] for i in range(3) for r in results)


def solution(mesh):
    shape = (mesh.shape["dp"] // 2, 2, mesh.shape["mp"] // 2, 2)
    inner = Mesh(np.asarray(mesh.devices).reshape(shape), ("far", "near", "y", "c"))
    dp = ("far", "near")
    mp = ("y", "c")
    params = (
        P(mp, dp),
        P(dp, mp),
        P(None, dp, None, mp),
        P(None, mp, dp),
        P(None, dp, None, mp),
        P(None, mp, dp),
        P(None, dp + mp),
    )
    ids = (P(None, dp, None), P(None, dp, None), P(None, dp), P(None, dp))
    return jax.shard_map(
        on_device,
        mesh=inner,
        in_specs=ids + params * 3,
        out_specs=(P(), P()) + params * 3,
        check_vma=False,
    )
```

```python
import jax
import jax.numpy as jnp
import numpy as np
from jax import lax
from jax.experimental.layout import Layout, with_layout_constraint
from jax.sharding import Mesh
from jax.sharding import PartitionSpec as P

DK = 64
STEP = 10


norm_eps = 1e-06
clip_limit = 0.05
step_rates = (0.4, 0.02, 0.02, 0.1, 0.02, 0.02, 0.25)
beta_one = 0.9
beta_two = 0.999
adam_eps = 1e-08
decay = 0.01
masked = -1000000000.0

half = jnp.bfloat16


def spin(part, axis, shift):
    size = lax.axis_size(axis)
    return lax.ppermute(part, axis, [(i, (i + shift) % size) for i in range(size)])


def flip(part, axis, bit):
    size = lax.axis_size(axis)
    return lax.ppermute(part, axis, [(i, i ^ bit) for i in range(size)])


def plain(part):
    return with_layout_constraint(part, Layout(major_to_minor=tuple(range(part.ndim))))


def ordered(part, order):
    return with_layout_constraint(part, Layout(major_to_minor=order))


def gather_unit(part):
    return lax.all_gather(plain(part), ("y", "near", "far"), axis=0, tiled=True)


def halves(whole):
    rows = whole.shape[0] // 2
    return [whole[:rows], whole[rows:]]


def place(part, other, axis, bit):
    first = (lax.axis_index(axis) // bit) % 2 == 0
    return [jnp.where(first, part, other), jnp.where(first, other, part)]


def join_rows(part, axis, bit):
    part = plain(part)
    return jnp.concatenate(place(part, flip(part, axis, bit), axis, bit), axis=0)


def gather_pairs(part, row_first):
    bit = 1
    while bit < lax.axis_size("far"):
        part = join_rows(part, "far", bit)
        bit *= 2
    if not row_first:
        part = plain(join_rows(part, "near", 1))
        return place(part, flip(part, "y", 1), "y", 1)
    part = plain(part)
    both = plain(jnp.concatenate([part, flip(part, "y", 1)], axis=0))
    pairs = zip(halves(both), halves(flip(both, "near", 1)))
    own, other = [jnp.concatenate(place(p, q, "near", 1), axis=0) for p, q in pairs]
    return place(own, other, "y", 1)


def scatter_unit(blocks, whole):
    rows, columns = blocks[0][0].shape
    for k, pair in enumerate(blocks):
        for y, part in enumerate(pair):
            whole = lax.dynamic_update_slice(whole, plain(part), (y * rows, k * columns))
    part = lax.psum_scatter(
        plain(whole), ("y", "near", "far"), scatter_dimension=0, tiled=True
    )
    return part.astype(jnp.float32)


def choose(parts, axis):
    first = lax.axis_index(axis) == 0
    own = jnp.where(first, parts[0], parts[1]).astype(jnp.float32)
    sent = plain(jnp.where(first, parts[1], parts[0]))
    return own + flip(sent, axis, 1).astype(jnp.float32)


def chosen(parts):
    first = lax.axis_index("y") == 0
    parts = [plain(p) for p in parts]
    own = jnp.where(first, parts[0], parts[1])
    return own, flip(plain(jnp.where(first, parts[1], parts[0])), "y", 1)


def nearer(own, got):
    whole = (own.astype(jnp.float32) + got.astype(jnp.float32)).astype(half)
    rows = whole.shape[0] // 2
    mine = lax.axis_index("near")
    own = lax.dynamic_slice_in_dim(whole, mine * rows, rows)
    return own, flip(plain(lax.dynamic_slice_in_dim(whole, (1 - mine) * rows, rows)), "near", 1)


def farther(own, got):
    part = own.astype(jnp.float32) + got.astype(jnp.float32)
    bit = lax.axis_size("far") // 2
    while bit:
        part = split_rows(part.astype(half), "far", bit)
        bit //= 2
    return part


def split_rows(whole, axis, bit):
    rows = whole.shape[0] // 2
    mine = (lax.axis_index(axis) // bit) % 2
    own = lax.dynamic_slice_in_dim(whole, mine * rows, rows)
    sent = plain(lax.dynamic_slice_in_dim(whole, (1 - mine) * rows, rows))
    return own.astype(jnp.float32) + flip(sent, axis, bit).astype(jnp.float32)


def scatter_rows(part, kind):
    part = split_rows(part.astype(kind), "near", 1)
    bit = lax.axis_size("far") // 2
    while bit:
        part = split_rows(part.astype(kind), "far", bit)
        bit //= 2
    return part


def scatter_pairs(parts):
    return scatter_rows(choose([plain(p) for p in parts], "y"), half)


def total_over(value, axes):
    for axis in axes:
        bit = 1
        while bit < lax.axis_size(axis):
            value = value + flip(value, axis, bit)
            bit *= 2
    return value


def collect(own):
    return jnp.concatenate([own, spin(own, "c", 1)], axis=0)


def fold(part):
    rows = part.shape[0] // 2
    return part[:rows] + spin(part[rows:].astype(half), "c", 1).astype(jnp.float32)


def product(left, right):
    return jnp.dot(left, right, preferred_element_type=jnp.float32)


def product_left(left, right):
    return lax.dot_general(
        left, right, (((0,), (0,)), ((), ())), preferred_element_type=jnp.float32
    )


def product_right(left, right):
    return lax.dot_general(
        left, right, (((1,), (1,)), ((), ())), preferred_element_type=jnp.float32
    )


def rms_norm(stream, gain):
    return stream * lax.rsqrt(jnp.mean(stream * stream, axis=-1, keepdims=True) + norm_eps) * gain


def normalize(stream, gain):
    return rms_norm(stream, gain).astype(half)


def norm_back(stream, gain, grad):
    _, pull = jax.vjp(rms_norm, stream, gain)
    return pull(grad)


def heads(flat):
    return flat.reshape(flat.shape[0], -1, DK)


def score_block(query, key, bias):
    return (
        jnp.einsum("rhd,shd->hrs", heads(query), heads(key), preferred_element_type=jnp.float32)
        * 0.125
        + bias
    )


def attend(query, key, value, bias):
    scores = score_block(query, key, bias)
    peak = jnp.max(scores, axis=-1, keepdims=True)
    raw = jnp.exp(scores - peak)
    total = jnp.sum(raw, axis=-1, keepdims=True)
    probs = (raw / total).astype(half)
    mixed = jnp.einsum("hrs,shd->rhd", probs, heads(value), preferred_element_type=jnp.float32)
    mixed = mixed.reshape(query.shape[0], -1).astype(half)
    return mixed, peak + jnp.log(total)


def attend_back(query, key, value, lse, bias, d_mixed):
    rows = query.shape[0]
    cols = key.shape[0]
    d_heads = heads(d_mixed)
    probs = jnp.exp(score_block(query, key, bias) - lse)
    d_value = jnp.einsum(
        "hrs,rhd->shd", probs.astype(half), d_heads, preferred_element_type=jnp.float32
    )
    d_probs = jnp.einsum("rhd,shd->hrs", d_heads, heads(value), preferred_element_type=jnp.float32)
    d_scores = (probs * (d_probs - jnp.sum(probs * d_probs, axis=-1, keepdims=True))).astype(half)
    d_query = (
        jnp.einsum("hrs,shd->rhd", d_scores, heads(key), preferred_element_type=jnp.float32) * 0.125
    )
    d_key = (
        jnp.einsum("hrs,rhd->shd", d_scores, heads(query), preferred_element_type=jnp.float32)
        * 0.125
    )
    return (
        d_query.reshape(rows, -1).astype(half),
        d_key.reshape(cols, -1).astype(half),
        d_value.reshape(cols, -1).astype(half),
    )


def self_attention(x_in, blocks, bias):
    part = 0.0
    kept = []
    for block in blocks:
        width = block.shape[1] // 4
        qkv = product(x_in, block[:, : 3 * width]).astype(half)
        query, key, value = qkv[:, :width], qkv[:, width : 2 * width], qkv[:, 2 * width :]
        mixed, lse = attend(query, key, value, bias)
        part = part + product_right(mixed, block[:, 3 * width :])
        kept.append((query, key, value, lse, mixed))
    return part, kept


def self_attention_back(x_in, blocks, bias, kept, d_full):
    d_in = 0.0
    grads = []
    for block, (query, key, value, lse, mixed) in zip(blocks, kept):
        width = block.shape[1] // 4
        g_out = product_left(d_full, mixed).astype(half)
        d_mixed = product(d_full, block[:, 3 * width :]).astype(half)
        d_qkv = jnp.concatenate(attend_back(query, key, value, lse, bias, d_mixed), axis=1)
        g_in = product_left(x_in, d_qkv).astype(half)
        grads.append(jnp.concatenate([g_in, g_out], axis=1))
        d_in = d_in + product_right(d_qkv, block[:, : 3 * width])
    return grads, d_in


def cross_attention(x_in, x_keys, blocks, bias):
    part = 0.0
    kept = []
    for block in blocks:
        width = block.shape[1] // 4
        query = product(x_in, block[:, :width]).astype(half)
        pair = product(x_keys, block[:, width : 3 * width]).astype(half)
        key, value = pair[:, :width], pair[:, width:]
        mixed, lse = attend(query, key, value, bias)
        part = part + product_right(mixed, block[:, 3 * width :])
        kept.append((query, key, value, lse, mixed))
    return part, kept


def cross_attention_back(x_in, x_keys, blocks, bias, kept, d_full):
    d_in = 0.0
    d_keys = 0.0
    grads = []
    for block, (query, key, value, lse, mixed) in zip(blocks, kept):
        width = block.shape[1] // 4
        g_out = product_left(d_full, mixed).astype(half)
        d_mixed = product(d_full, block[:, 3 * width :]).astype(half)
        d_query, d_key, d_value = attend_back(query, key, value, lse, bias, d_mixed)
        d_pair = jnp.concatenate([d_key, d_value], axis=1)
        g_query = product_left(x_in, d_query).astype(half)
        g_pair = product_left(x_keys, d_pair).astype(half)
        grads.append(jnp.concatenate([g_query, g_pair, g_out], axis=1))
        d_in = d_in + product_right(d_query, block[:, :width])
        d_keys = d_keys + product_right(d_pair, block[:, width : 3 * width])
    return grads, d_in, d_keys


def gated(gate, upper):
    return jax.nn.gelu(gate, approximate=True) * upper


def expand(x_in, gates, uppers, downs):
    part = 0.0
    kept = []
    for w_gate, w_upper, w_down in zip(gates, uppers, downs):
        gate = product(x_in, w_gate)
        upper = product(x_in, w_upper)
        hidden = gated(gate, upper).astype(half)
        part = part + product_right(hidden, w_down)
        kept.append((gate, upper, hidden))
    return part, kept


def expand_back(x_in, gates, uppers, downs, kept, d_full):
    d_in = 0.0
    g_gates, g_uppers, g_downs = [], [], []
    for w_gate, w_upper, w_down, (gate, upper, hidden) in zip(gates, uppers, downs, kept):
        g_downs.append(product_left(d_full, hidden).astype(half))
        _, pull = jax.vjp(gated, gate, upper)
        d_gate, d_upper = pull(product(d_full, w_down))
        d_gate = d_gate.astype(half)
        d_upper = d_upper.astype(half)
        g_gates.append(product_left(x_in, d_gate).astype(half))
        g_uppers.append(product_left(x_in, d_upper).astype(half))
        d_in = d_in + product_right(d_gate, w_gate) + product_right(d_upper, w_upper)
    return g_gates, g_uppers, g_downs, d_in


def adam(weight, grad, first, second, step_rate):
    first = beta_one * first + (1 - beta_one) * grad
    second = beta_two * second + (1 - beta_two) * grad * grad
    step_size = first / (1 - beta_one**STEP) / (jnp.sqrt(second / (1 - beta_two**STEP)) + adam_eps)
    return (weight - step_rate * (step_size + decay * weight), first, second)


def own_part(whole, rows):
    return lax.dynamic_slice_in_dim(whole, lax.axis_index("c") * rows, rows)


def positions(rows):
    core = lax.axis_index("c")
    near = jnp.arange(rows, dtype=jnp.int32)
    return jnp.concatenate([core * rows + near, (1 - core) * rows + near])


def on_device(*args):
    source_ids, target_ids, source_lengths, target_lengths = args[:4]
    masters, firsts, seconds = args[4:11], args[11:18], args[18:25]
    embedding, unembedding, attention_in, attention_out, feed_in, feed_out, norm_gains = masters
    row = lax.axis_index("y")
    core = lax.axis_index("c")
    everywhere = ("near", "far", "y", "c")

    vocab_rows = embedding.shape[0]
    table_pair = jnp.concatenate([embedding.T.astype(half), unembedding.astype(half)], axis=1)
    near = jnp.arange(vocab_rows, dtype=jnp.int32)
    vocab_ids = jnp.concatenate(
        [(y * 2 + (core ^ step)) * vocab_rows + near for step in (0, 1) for y in (0, 1)]
    )

    own_count = jnp.sum(target_lengths).astype(jnp.float32)
    gain_part = jnp.concatenate(
        [norm_gains, jnp.full((1, norm_gains.shape[1]), own_count, jnp.float32)]
    )
    gain_part = lax.all_gather(gain_part, everywhere)
    count = jnp.sum(gain_part[::4, -1, 0])
    gains = gain_part[:, :-1].swapaxes(0, 1).reshape(norm_gains.shape[0], -1)

    hidden_rows = feed_out.shape[1]
    spare = ((0, 0), (0, -hidden_rows % 128))

    def attention_unit(layer):
        w_in = attention_in[layer].astype(half)
        w_in = w_in.reshape(w_in.shape[0], -1)
        return [w_in, attention_out[layer].T.astype(half)]

    def feed_units(layer):
        return [
            jnp.pad(feed_in[layer, :, 0].astype(half), spare),
            jnp.pad(feed_in[layer, :, 1].astype(half), spare),
            jnp.pad(feed_out[layer].T.astype(half), spare),
        ]

    third = hidden_rows + spare[1][1]

    def thirds(blocks, start):
        return [
            [b[:, start + k * third : start + (k + 1) * third] for b in blocks] for k in range(3)
        ]

    first = plain(jnp.concatenate(feed_units(0) + [table_pair], axis=1))
    attn = [plain(jnp.concatenate(attention_unit(layer), axis=1)) for layer in range(3)]
    attn, gains = lax.optimization_barrier((attn, gains))
    first = gather_unit(first)
    second = halves(gather_unit(jnp.concatenate(feed_units(1), axis=1)))
    attn = [gather_pairs(a, row_first) for a, row_first in zip(attn, (False, True, False))]
    fills = (jnp.minimum(jnp.sum(target_lengths), 0), jnp.minimum(jnp.sum(source_lengths), 0))
    blanks = [jnp.full((first.shape[0], 2 * third), f.astype(half)) for f in fills]
    first, attn, blanks = lax.optimization_barrier((first, attn, blanks))
    first = halves(first)
    edge = first[0].shape[1] - 2 * vocab_rows
    feed = (thirds(first, 0), thirds(second, 0))
    near_pair = jnp.concatenate([b[:, edge:] for b in first], axis=1)
    table_pairs = [near_pair, flip(plain(near_pair), "c", 1)]
    table_pairs = [p[:, k * vocab_rows :][:, :vocab_rows] for p in table_pairs for k in range(4)]
    table_t = jnp.concatenate(table_pairs[::2], axis=1)
    w_head = jnp.concatenate(table_pairs[1::2], axis=1)

    source = lax.dynamic_index_in_dim(source_ids, row, 0, False)[0]
    target = lax.dynamic_index_in_dim(target_ids, row, 0, False)[0]
    source_len = lax.dynamic_index_in_dim(source_lengths, row, 0, False)[0]
    target_len = lax.dynamic_index_in_dim(target_lengths, row, 0, False)[0]
    src_rows = source.shape[0] // 2
    tgt_rows = target.shape[0] // 2
    src_pos = positions(src_rows)
    tgt_pos = positions(tgt_rows)
    key_bias = jnp.where(src_pos < source_len, 0.0, masked)[None, None, :]
    causal = jnp.where(tgt_pos[:, None] >= tgt_pos[None, :], 0.0, masked)[None]
    shifted = jnp.concatenate([jnp.zeros((1,), jnp.int32), target[:-1]])
    source_hot = (own_part(source, src_rows)[:, None] == vocab_ids[None, :]).astype(half)
    target_hot = (own_part(shifted, tgt_rows)[:, None] == vocab_ids[None, :]).astype(half)
    hits = own_part(target, tgt_rows)[:, None] == vocab_ids[None, :]

    src_embed = product_right(source_hot, table_t)
    src_norm_a = collect(normalize(src_embed, gains[0]))
    part, keep_src_a = self_attention(src_norm_a, attn[0], key_bias)
    src_mid = src_embed + fold(part)
    src_norm_b = collect(normalize(src_mid, gains[1]))
    part, keep_src_b = expand(src_norm_b, *feed[0])
    src_top = src_mid + fold(part)
    encoded = collect(normalize(src_top, gains[2]))

    tgt_embed = product_right(target_hot, table_t)
    tgt_norm_a = collect(normalize(tgt_embed, gains[3]))
    part, keep_tgt_a = self_attention(tgt_norm_a, attn[1], causal)
    tgt_self = tgt_embed + fold(part)
    tgt_norm_b = collect(normalize(tgt_self, gains[4]))
    part, keep_tgt_b = cross_attention(tgt_norm_b, encoded, attn[2], key_bias)
    tgt_cross = tgt_self + fold(part)
    tgt_norm_c = collect(normalize(tgt_cross, gains[5]))
    part, keep_tgt_c = expand(tgt_norm_c, *feed[1])
    tgt_top = tgt_cross + fold(part)
    tgt_norm_d = normalize(tgt_top, gains[6])

    logits = product(tgt_norm_d, w_head)
    peak = jnp.max(logits, axis=-1, keepdims=True)
    lse = peak + jnp.log(jnp.sum(jnp.exp(logits - peak), axis=-1, keepdims=True))
    picked = jnp.sum(jnp.where(hits, logits, 0.0), axis=-1, keepdims=True)
    weight = (tgt_pos[:tgt_rows] < target_len).astype(jnp.float32)[:, None] / count
    own_loss = jnp.sum((lse - picked) * weight)
    d_logits = ((jnp.exp(logits - lse) - hits.astype(jnp.float32)) * weight).astype(half)
    g_head = product_left(tgt_norm_d, d_logits).astype(half)

    d_tgt, gain_six = norm_back(tgt_top, gains[6], product_right(d_logits, w_head))
    *feed_one, d_in = expand_back(tgt_norm_c, *feed[1], keep_tgt_c, collect(d_tgt.astype(half)))
    early = [chosen(feed_one[2])]
    feed_one = scatter_unit(feed_one[:2], blanks[1])
    d_more, gain_five = norm_back(tgt_cross, gains[5], fold(d_in))
    d_tgt = d_tgt + d_more
    attn_two, d_query, d_keys = cross_attention_back(
        tgt_norm_b, encoded, attn[2], key_bias, keep_tgt_b, collect(d_tgt.astype(half))
    )
    early.append(chosen(attn_two))
    d_encoded = fold(d_keys)
    d_more, gain_four = norm_back(tgt_self, gains[4], fold(d_query))
    d_tgt = d_tgt + d_more
    attn_one, d_in = self_attention_back(
        tgt_norm_a, attn[1], causal, keep_tgt_a, collect(d_tgt.astype(half))
    )
    early.append(chosen(attn_one))
    d_more, gain_three = norm_back(tgt_embed, gains[3], fold(d_in))
    d_tgt = d_tgt + d_more

    d_src, gain_two = norm_back(src_top, gains[2], d_encoded)
    *feed_zero, d_in = expand_back(src_norm_b, *feed[0], keep_src_b, collect(d_src.astype(half)))
    early, d_in = lax.optimization_barrier((early, d_in))
    early = [nearer(*e) for e in early] + [chosen(feed_zero[2])]
    feed_zero = scatter_unit(feed_zero[:2], blanks[0])
    d_more, gain_one = norm_back(src_mid, gains[1], fold(d_in))
    d_src = d_src + d_more
    attn_zero, d_in = self_attention_back(
        src_norm_a, attn[0], key_bias, keep_src_a, collect(d_src.astype(half))
    )
    early, attn_zero = lax.optimization_barrier((early, attn_zero))
    down_one, attn_two, attn_one = [farther(*e) for e in early[:3]]
    down_zero = farther(*nearer(*early[3]))
    attn_zero = scatter_pairs(attn_zero)
    d_more, gain_zero = norm_back(src_embed, gains[0], fold(d_in))
    d_src = d_src + d_more

    g_table = product_left(d_src.astype(half), source_hot)
    g_table = (g_table + product_left(d_tgt.astype(half), target_hot)).astype(half)
    pairs = [g[:, k * vocab_rows :][:, :vocab_rows] for k in range(4) for g in (g_table, g_head)]
    pairs = [jnp.concatenate(pairs[k : k + 2], axis=1) for k in range(0, 8, 2)]
    pairs = jnp.concatenate([plain(p) for p in pairs], axis=0)
    rows = pairs.shape[0] // 2
    pairs = pairs[:rows].astype(jnp.float32) + flip(pairs[rows:], "c", 1).astype(jnp.float32)
    pairs = pairs.astype(half)
    pair_grad = scatter_pairs([pairs[: rows // 2], pairs[rows // 2 :]])

    g_gains = jnp.stack([gain_zero, gain_one, gain_two, gain_three, gain_four, gain_five, gain_six])
    g_gains = scatter_rows(g_gains.T, jnp.float32)
    g_gains = split_rows(split_rows(g_gains, "y", 1), "c", 1).T

    width = attention_out.shape[1]
    attn_grads = [attn_zero, attn_one, attn_two]
    units = [pair_grad, *attn_grads, feed_zero, feed_one, down_zero, down_one]
    squares = sum(jnp.sum(g * g) for g in units) + jnp.sum(g_gains * g_gains)
    squares, loss = total_over(jnp.stack([squares, own_loss]), everywhere)
    attn_in = [g[:, : 3 * width].reshape(-1, 3, width) for g in attn_grads]
    gates_uppers = [
        g.reshape(-1, 2, third)[..., :hidden_rows] for g in (feed_zero, feed_one)
    ]
    downs = [g[:, :hidden_rows].T for g in (down_zero, down_one)]
    grads = (
        plain(pair_grad[:, :vocab_rows].T),
        plain(pair_grad[:, vocab_rows:]),
        ordered(jnp.stack(attn_in), (0, 2, 1, 3)),
        plain(jnp.stack([g[:, 3 * width :].T for g in attn_grads])),
        plain(jnp.stack(gates_uppers)),
        ordered(jnp.stack(downs), (0, 2, 1)),
        g_gains,
    )
    grad_norm = jnp.sqrt(squares)
    scale = jnp.minimum(1.0, clip_limit / grad_norm)
    results = [
        adam(w, g * scale, m, v, r)
        for w, g, m, v, r in zip(masters, grads, firsts, seconds, step_rates)
    ]
    return (loss, grad_norm) + tuple(r[i] for i in range(3) for r in results)


def solution(mesh):
    shape = (mesh.shape["dp"] // 2, 2, mesh.shape["mp"] // 2, 2)
    inner = Mesh(np.asarray(mesh.devices).reshape(shape), ("far", "near", "y", "c"))
    dp = ("far", "near")
    mp = ("y", "c")
    params = (
        P(mp, dp),
        P(dp, mp),
        P(None, dp, None, mp),
        P(None, mp, dp),
        P(None, dp, None, mp),
        P(None, mp, dp),
        P(None, dp + mp),
    )
    ids = (P(None, dp, None), P(None, dp, None), P(None, dp), P(None, dp))
    return jax.shard_map(
        on_device,
        mesh=inner,
        in_specs=ids + params * 3,
        out_specs=(P(), P()) + params * 3,
        check_vma=False,
    )
```
